512 devices in a mesh: sta: 16 (over x_lo, y, core), src: 32 (over z, x_hi).
Axes of the slice: x: 4 (x_hi: 2, x_lo: 2; x = x_hi * 2 + x_lo), y: 4, z: 16, core: 2. Of those that a mesh axis runs over, the one named last changes fastest.
Arguments:
- features: bfloat16 [512, 1024, 128], P('sta', 'src'), may hold values from -6 to 6
- station_lists: int32 [512, 16], replicated, may hold values from 0 to 511, as said below
- station_counts: int32 [512], replicated, may hold values from 1 to 16
- source_lists: int32 [1024, 16], replicated, may hold values from 0 to 1023, as said below
- source_counts: int32 [1024], replicated, may hold values from 1 to 16
- picks: int32 [2, 512], P(None, 'sta'), may hold values 0 or 1
- targets: float32 [2, 1024], P(None, 'src'), may hold values from 0 to 1
- layer_weights: bfloat16 [2, 3, 64, 64], replicated, may hold values from -0.75 to 0.75
- readout_vector: bfloat16 [64], replicated, may hold values from -0.75 to 0.75
Outputs:
- likelihood: float32 [2, 1024], P(None, 'src')
- feature_grad: bfloat16 [512, 1024, 128], P('sta', 'src')
- weight_grad: float32 [2, 3, 64, 64], replicated
- vector_grad: float32 [64], replicated
The draws below stay inside these ranges and needn't reach their ends.
Inputs may be any that keep to these rules, and one draw needn't show every extreme that they name: `station_lists`: every entry of a station's list lies within 16 rows of that station; entries past its count are padding. `source_lists`: every entry of a source node's list lies within 16 rows of that source node; entries past its count are padding.
All inputs are finite; a program needn't handle non-finite values. No bound on the sum of `picks` on one device may be relied on, other than what follows from the above.
Results may differ from the reference program's by a relative error of at most 0.015.
Values may be sent and summed in bfloat16 or wider, within the bound.
No kernel may reach another device: no remote copies, remote signals or barrier semaphores. Data moves between devices by JAX's collectives and lax.ppermute only.
A program may use at most 64 MiB of HBM per device.

```python
import jax
import jax.numpy as jnp
from jax import lax

F = 64
W = 2
LAYERS = 2
KS = 16
KR = 16
HW = 16
NSTA = 512
NSRC = 1024


def neighbour_table(key, row_count, list_width):
    key_span, key_sign = jax.random.split(key)
    span_sizes = jax.random.randint(key_span, (row_count, list_width), 1, HW + 1)
    sign_bits = jax.random.randint(key_sign, (row_count, list_width), 0, 2) * 2 - 1
    offsets = span_sizes * sign_bits
    own_rows = jnp.arange(row_count, dtype=jnp.int32)[:, None]
    edge_step = jnp.where(own_rows % 2 == 0, HW, -HW)
    offsets = offsets.at[:, 0:1].set(edge_step)
    return jnp.clip(own_rows + offsets, 0, row_count - 1).astype(jnp.int32)


def neighbour_counts(key, row_count, list_width):
    counts = jax.random.randint(key, (row_count,), 1, list_width + 1)
    return counts.at[0].set(list_width).at[1].set(1).astype(jnp.int32)


def draw_station_lists(key, part):
    return neighbour_table(jax.random.fold_in(key, 11), NSTA, KS)


def draw_station_counts(key, part):
    return neighbour_counts(jax.random.fold_in(key, 12), NSTA, KS)


def draw_source_lists(key, part):
    return neighbour_table(jax.random.fold_in(key, 13), NSRC, KR)


def draw_source_counts(key, part):
    return neighbour_counts(jax.random.fold_in(key, 14), NSRC, KR)


def plant(drawn, own_key, least, largest):
    dims = drawn.shape
    spot = [jax.random.randint(jax.random.fold_in(own_key, axis), (), 0, dims[axis]) for axis in range(len(dims))]
    drawn = drawn.at[tuple(spot)].set(least)
    longest = dims.index(max(dims))
    spot[longest] = (spot[longest] + 1) % dims[longest]
    return drawn.at[tuple(spot)].set(largest)


def steps_of(own_key, shape, shards, low, high):
    loudness, own = 1.0, jax.random.fold_in(own_key, 6)
    for dim, blocks in shards:
        draws = jnp.exp(jax.random.uniform(jax.random.fold_in(own, dim), (blocks,), jnp.float32, low / len(shards), high / len(shards)))
        loudness = loudness * jnp.repeat(draws, shape[dim] // blocks).reshape([-1 if axis == dim else 1 for axis in range(len(shape))])
    return loudness


def bell_draw(rng, extent, width, limit, pieces=(), kind=jnp.bfloat16):
    drawn = jax.random.normal(rng, extent, jnp.float32) * width
    if len(pieces) > 0:
        drawn = steps_of(rng, extent, pieces, -0.22, 0.18) * drawn
    return jnp.clip(drawn, min=-limit, max=limit).astype(kind)


def setup_inputs(seed: int = 0) -> dict:
    key_list = jax.random.split(jax.random.key(seed), 10)
    return {
        "features": bell_draw(key_list[0], (NSTA, NSRC, W * F), 1.0, 6.0, ((0, 16), (1, 32))),
        "station_lists": draw_station_lists(jax.random.fold_in(key_list[9], 71), 0),
        "station_counts": draw_station_counts(jax.random.fold_in(key_list[9], 71), 0),
        "source_lists": draw_source_lists(jax.random.fold_in(key_list[9], 71), 0),
        "source_counts": draw_source_counts(jax.random.fold_in(key_list[9], 71), 0),
        "picks": plant((jax.random.randint(key_list[5], (W, NSTA), 0, 2) < 1).astype(jnp.int32), jax.random.fold_in(key_list[5], 1), 0, 1),
        "targets": jnp.clip(1.0 * jax.random.uniform(key_list[6], (W, NSRC), jnp.float32) ** steps_of(key_list[6], (W, NSRC), ((1, 32),), -0.2, 0.2), 0.0, 1.0),
        "layer_weights": bell_draw(key_list[7], (LAYERS, 3, F, F), F ** -0.5, 0.75),
        "readout_vector": bell_draw(key_list[8], (F,), F ** -0.5, 0.75),
    }


def window_product(values, matrix):
    feature = matrix.shape[0]
    flat = values.reshape(-1, feature)
    return jnp.dot(flat, matrix, preferred_element_type=jnp.float32).reshape(values.shape)

def station_mix(states, lists, counts):
    running = jnp.zeros(states.shape, jnp.float32)
    for column in range(KS):
        kept_rows = (column < counts).astype(jnp.float32)[:, None, None]
        running = running + kept_rows * states[lists[:, column]].astype(jnp.float32)
    return running / counts.astype(jnp.float32)[:, None, None]

def source_mix(states, lists, counts):
    running = jnp.zeros(states.shape, jnp.float32)
    for column in range(KR):
        kept_rows = (column < counts).astype(jnp.float32)[None, :, None]
        running = running + kept_rows * states[:, lists[:, column]].astype(jnp.float32)
    return running / counts.astype(jnp.float32)[None, :, None]

def station_back(cotangent, lists, counts):
    running = jnp.zeros(cotangent.shape, jnp.float32)
    for column in range(KS):
        kept_rows = (column < counts).astype(jnp.float32)[:, None, None]
        running = running.at[lists[:, column]].add(kept_rows * cotangent.astype(jnp.float32))
    return running

def source_back(cotangent, lists, counts):
    running = jnp.zeros(cotangent.shape, jnp.float32)
    for column in range(KR):
        kept_rows = (column < counts).astype(jnp.float32)[None, :, None]
        running = running.at[:, lists[:, column]].add(kept_rows * cotangent.astype(jnp.float32))
    return running

def layer_parts(states, weights, station_lists, station_counts, source_lists, source_counts):
    sta_mean = station_mix(states, station_lists, station_counts).astype(jnp.bfloat16)
    src_mean = source_mix(states, source_lists, source_counts).astype(jnp.bfloat16)
    linear = window_product(states, weights[0]) + window_product(sta_mean, weights[1]) + window_product(src_mean, weights[2])
    return (sta_mean, src_mean, jnp.tanh(linear))

def outer_sum(left, right, feature):
    return jnp.dot(left.reshape(-1, feature).T, right.reshape(-1, feature), preferred_element_type=jnp.float32)

def reference(features, station_lists, station_counts, source_lists, source_counts, picks, targets, layer_weights, readout_vector):
    feature = layer_weights.shape[-1]
    windows = features.shape[2] // feature
    states = features
    history = []
    for layer_idx in range(LAYERS):
        history.append(states)
        sta_mean, src_mean, squashed = layer_parts(states, layer_weights[layer_idx], station_lists, station_counts, source_lists, source_counts)
        states = (states.astype(jnp.float32) + squashed).astype(jnp.bfloat16)
    score = jnp.dot(states.reshape(-1, feature), readout_vector, preferred_element_type=jnp.float32)
    score = score.reshape(NSTA, NSRC, windows)
    picked = picks.astype(jnp.float32)
    root = jnp.sqrt(jnp.maximum(lax.optimization_barrier(jnp.sum(picked, axis=1)), 1.0))
    summed = lax.optimization_barrier(jnp.sum(picked.T[:, None, :] * score, axis=0)).T
    likelihood = summed / root[:, None]
    error = jax.nn.sigmoid(likelihood) - targets
    d_score = (picked.T[:, None, :] * error.T[None, :, :]).astype(jnp.bfloat16)
    v_sum = jnp.einsum('nw,nwf->f', d_score.reshape(-1, windows).astype(jnp.float32), states.reshape(-1, windows, feature).astype(jnp.float32), precision=lax.Precision.HIGHEST)
    grad = (d_score.astype(jnp.float32)[..., None] * readout_vector.astype(jnp.float32)).reshape(states.shape)
    w_rows = []
    for layer_idx in reversed(range(LAYERS)):
        weights = layer_weights[layer_idx]
        before = history[layer_idx]
        sta_mean, src_mean, squashed = layer_parts(before, weights, station_lists, station_counts, source_lists, source_counts)
        delta = (grad * (1.0 - squashed * squashed)).astype(jnp.bfloat16)
        w_rows.append(jnp.stack([outer_sum(before, delta, feature), outer_sum(sta_mean, delta, feature), outer_sum(src_mean, delta, feature)]))
        u_sta = (window_product(delta, weights[1].T) / station_counts.astype(jnp.float32)[:, None, None]).astype(jnp.bfloat16)
        u_src = (window_product(delta, weights[2].T) / source_counts.astype(jnp.float32)[None, :, None]).astype(jnp.bfloat16)
        grad = grad + window_product(delta, weights[0].T) + station_back(u_sta, station_lists, station_counts) + source_back(u_src, source_lists, source_counts)
    w_sum = jnp.stack(w_rows[::-1])
    factor = 1.0 / jnp.sqrt(jnp.float32(NSTA) * jnp.float32(NSRC))
    return (likelihood, grad.astype(jnp.bfloat16), w_sum * factor, v_sum * factor)
```

```python
import jax
import jax.numpy as jnp
from jax import lax
from jax.experimental import pallas as pl
from jax.experimental.pallas import tpu as pltpu
from jax.sharding import Mesh
from jax.sharding import PartitionSpec as P

LAYERS = 2
HW = 16
BF = jnp.bfloat16
F32 = jnp.float32
PLANE = ("sta", "xh")
SRC = ("z", "xh")
NT = (((1,), (1,)), ((), ()))
TN = (((0,), (0,)), ((), ()))
VMEM_LIMIT = 40 * 1024 * 1024


def iota(shape, dim):
    return lax.broadcasted_iota(jnp.int32, shape, dim)


def dot(a, b):
    return jnp.dot(a, b, preferred_element_type=F32)


def dot_nt(a, b, precision=None):
    return lax.dot_general(a, b, NT, precision=precision, preferred_element_type=F32)


def onehot(mask):
    return jnp.where(mask, 1.0, 0.0).astype(BF)


def call(body, outs, *args):
    vm = pl.BlockSpec(memory_space=pltpu.VMEM)
    return pl.pallas_call(
        body,
        out_shape=[jax.ShapeDtypeStruct(s, d) for s, d in outs],
        in_specs=[vm] * len(args),
        out_specs=[vm] * len(outs),
        compiler_params=pltpu.CompilerParams(vmem_limit_bytes=VMEM_LIMIT),
    )(*args)


def count_rows(counts_ref, first, rows):
    total = counts_ref.shape[1]
    hit = onehot(iota((rows, total), 1) == iota((rows, total), 0) + first)
    every = jnp.broadcast_to(counts_ref[...].astype(F32), (128, total)).astype(BF)
    return dot_nt(hit, every)


def list_counts(lists, counts, first, span):
    rows = lists.shape[0]
    shifted = lists - first
    cols = iota((rows, span), 1)
    acc = jnp.zeros((rows, span), F32)
    for k in range(lists.shape[1]):
        hit = (shifted[:, k : k + 1] == cols) & (counts[:, :span] > k)
        acc = acc + jnp.where(hit, 1.0, 0.0)
    return acc.astype(BF)


def mixes(lists_ref, counts_ref, first, own):
    total = lists_ref.shape[0]
    lo = pl.multiple_of(jnp.maximum(first - HW, 0), HW)
    mid = pl.multiple_of(first, HW)
    hi = pl.multiple_of(jnp.minimum(first + own, total - HW), HW)
    mine = lists_ref[pl.ds(mid, own), :]
    wide = jnp.concatenate([lists_ref[pl.ds(lo, HW), :], mine, lists_ref[pl.ds(hi, HW), :]], 0)
    own_counts = count_rows(counts_ref, first, own)
    wide_counts = count_rows(counts_ref, first - HW, own + 2 * HW)
    span = own + 2 * HW
    gather = list_counts(mine, own_counts, first - HW, span)
    scatter = list_counts(wide, wide_counts, first, own)
    return gather, scatter, own_counts


def prep_body(sta_rows, src_rows, *refs):
    (slists, scounts, rlists, rcounts, picks, targets, weights, readout) = refs[:8]
    (sk, tk, rk, qk, sinv, rinv, wf, wb, px, cnt, tgt, rl) = refs[8:]
    sta_first = lax.axis_index("sta") * sta_rows
    src_first = (lax.axis_index("z") * lax.axis_size("xh") + lax.axis_index("xh")) * src_rows
    feature = weights.shape[-1]
    channels = 2 * feature

    gather, scatter, own_counts = mixes(slists, scounts, sta_first, sta_rows)
    ext = sta_rows + 2 * HW
    spread_cols = onehot(iota((ext, ext * HW), 1) >> 4 == iota((ext, ext * HW), 0))
    step = 128
    per = step // HW
    lane_mask = (iota((step, ext * HW), 0) & 15) == (iota((step, ext * HW), 1) & 15)
    for part in range(sta_rows * HW // step):
        pick_rows = onehot((iota((step, sta_rows), 0) >> 4) + part * per == iota((step, sta_rows), 1))
        for source, target, form in ((gather, sk, dot), (scatter, tk, dot_nt)):
            rows = form(pick_rows, source).astype(BF)
            full = dot(rows, spread_cols)
            target[part * step : (part + 1) * step, :] = jnp.where(lane_mask, full, 0.0).astype(BF)
        inverse = 1.0 / dot(pick_rows, own_counts.astype(BF))
        sinv[part * step : (part + 1) * step, :] = inverse

    gather, scatter, own_counts = mixes(rlists, rcounts, src_first, src_rows)
    ext = src_rows + 2 * HW
    rows_n, cols_n = 4 * src_rows, 4 * ext
    pick_rows = onehot((iota((rows_n, src_rows), 0) & (src_rows - 1)) == iota((rows_n, src_rows), 1))
    spread_cols = onehot((iota((ext, cols_n), 1) & (ext - 1)) == iota((ext, cols_n), 0))
    block_mask = (iota((rows_n, cols_n), 0) >> 5) == (iota((rows_n, cols_n), 1) >> 6)
    for source, target, form in ((gather, rk, dot), (scatter, qk, dot_nt)):
        full = dot(form(pick_rows, source).astype(BF), spread_cols)
        target[...] = jnp.where(block_mask, full, 0.0).astype(BF)
    rinv[...] = 1.0 / dot(pick_rows, own_counts.astype(BF))

    twice = onehot((iota((feature, channels), 1) & (feature - 1)) == iota((feature, channels), 0))
    unit = onehot(iota((feature, feature), 0) == iota((feature, feature), 1))
    left = iota((feature, channels), 1) < feature
    for layer in range(LAYERS):
        for which in range(3):
            matrix = weights[layer, which]
            plain = dot(matrix, twice)
            turned = dot_nt(unit, jnp.concatenate([matrix, matrix], 0))
            at = which * channels
            wf[layer, at : at + feature, :] = jnp.where(left, plain, 0.0).astype(BF)
            wf[layer, at + feature : at + channels, :] = jnp.where(left, 0.0, plain).astype(BF)
            wb[layer, :feature, at : at + channels] = jnp.where(left, turned, 0.0).astype(BF)
            wb[layer, feature:, at : at + channels] = jnp.where(left, 0.0, turned).astype(BF)
    rl[...] = dot(jnp.broadcast_to(readout[...].astype(F32), (16, feature)).astype(BF), twice)[:8]

    window = iota((16, sta_rows), 0)
    picked = picks[...].astype(F32)
    rows = jnp.where(window == 0, picked[0:1, :], jnp.where(window == 1, picked[1:2, :], 0.0)).astype(BF)
    choose = onehot((iota((16, channels), 1) >> 6) == iota((16, channels), 0))
    chunk = 256
    for part in range(sta_rows * src_rows // chunk):
        at = part * chunk
        own = onehot((iota((chunk, sta_rows), 0) + at) >> 5 == iota((chunk, sta_rows), 1))
        wide = dot(dot_nt(own, rows).astype(BF), choose).astype(BF)
        span = chunk // src_rows
        px[part * span : (part + 1) * span] = wide.reshape(span, src_rows, channels)
    cnt[...] = dot(rows, jnp.ones((sta_rows, channels), BF))[:8]
    line = iota((8, src_rows), 0)
    aims = targets[...]
    tgt[...] = jnp.where(line == 0, aims[0:1, :], jnp.where(line == 1, aims[1:2, :], 0.0))


def edge_body(x, hi, lo, right, left):
    store_edges(x, x, hi, lo, right, left)


def store_edges(rows, cols, hi, lo, right, left):
    hi[...] = rows[rows.shape[0] - HW :]
    lo[...] = rows[:HW]
    right[...] = cols[:, cols.shape[1] - HW :]
    left[...] = cols[:, :HW]


def mix_sta(mix, up, own, down):
    span = own.shape[0] + 2 * HW
    parts = []
    for g in range(own.shape[1] // HW):
        cut = slice(g * HW, (g + 1) * HW)
        parts.append(
            jnp.concatenate([up[:, cut], own[:, cut], down[:, cut]], 0).reshape(span * HW, 128)
        )
    out = dot(mix[...], jnp.concatenate(parts, 1))
    return [out[:, g * 128 : (g + 1) * 128] for g in range(len(parts))]


def mix_src(mix, left, own, right, first):
    parts = []
    for at in (first, first + 4):
        cut = slice(at, at + 4)
        joined = jnp.concatenate([left[cut], own[cut], right[cut]], 1)
        parts.append(joined.reshape(4 * joined.shape[1], 128))
    out = dot(mix[...], jnp.concatenate(parts, 1))
    return jnp.concatenate([out[:, :128], out[:, 128:]], 0)


def forward_parts(h, up, down, left, right, sk, rk, sinv, rinv, wf, states, keep, layer):
    rows, cols, _ = h.shape
    for g, part in enumerate(mix_sta(sk, up, h, down)):
        mean = (part * sinv[...]).astype(BF).reshape(rows, HW, 128)
        states[:, g * HW : (g + 1) * HW, 128:256] = mean
    states[:, :, :128] = h[...]
    both = jnp.concatenate([rinv[...], rinv[...]], 0)
    for p in range(rows // 8):
        cut = slice(8 * p, 8 * p + 8)
        mean = (mix_src(rk, left, h, right, 8 * p) * both).astype(BF)
        states[cut, :, 256:384] = mean.reshape(8, cols, 128)
        z = dot(states[cut].reshape(8 * cols, 384), wf[layer])
        t = jnp.tanh(z)
        keep[cut] = (1.0 - t * t).reshape(8, cols, 128)
        before = h[cut].reshape(8 * cols, 128).astype(F32)
        yield cut, (before + t).astype(BF)


def forward0_body(h, up, down, left, right, sk, rk, sinv, rinv, wf, nxt, hi, lo, rgt, lft, states, keep):
    cols = h.shape[1]
    for cut, after in forward_parts(h, up, down, left, right, sk, rk, sinv, rinv, wf, states, keep, 0):
        nxt[cut] = after.reshape(8, cols, 128)
    store_edges(nxt, nxt, hi, lo, rgt, lft)


def forward1_body(h, up, down, left, right, sk, rk, sinv, rinv, wf, px, cnt, rl, states, keep, xsum, block):
    cols = h.shape[1]
    acc = jnp.zeros((cols, 128), F32)
    for cut, after in forward_parts(h, up, down, left, right, sk, rk, sinv, rinv, wf, states, keep, 1):
        part = after.astype(F32).reshape(8, cols, 128) * px[cut].astype(F32)
        acc = acc + jnp.sum(part, axis=0)
    xsum[...] = acc
    read = jnp.where((iota((8, 128), 1) >> 6) == iota((8, 128), 0), rl[...], 0.0)
    padded = jnp.concatenate([acc, jnp.zeros((128 - cols, 128), F32)], 0)
    sums = dot_nt(read, padded, precision=lax.Precision.HIGHEST)
    mixed = jnp.where(iota((8, 128), 1) < 64, sums, cnt[...])
    block[...] = jnp.broadcast_to(mixed[None], block.shape)


def backward_tail(make, q, states, wb, sinv, rinv, layer, delta, direct, usta, usrc, edges):
    rows, cols, _ = q.shape
    both = jnp.concatenate([rinv[...], rinv[...]], 0)
    for p in range(rows // 8):
        cut = slice(8 * p, 8 * p + 8)
        grad = make(p)
        d = (grad * q[cut].reshape(8 * cols, 128)).astype(BF)
        delta[8 * cols * p : 8 * cols * (p + 1), :] = d
        u = dot(d, wb[layer])
        direct[cut] = (grad + u[:, :128]).reshape(8, cols, 128)
        scale = sinv[8 * HW * p : 8 * HW * (p + 1), :].reshape(8, HW, 128)
        scale = jnp.concatenate([scale] * (cols // HW), 1)
        usta[cut] = (u[:, 128:256].reshape(8, cols, 128) * scale).astype(BF)
        usrc[cut] = (u[:, 256:384] * both).astype(BF).reshape(8, cols, 128)
    store_edges(usta, usrc, *edges)
    flat = states[...].reshape(rows * cols, 384)
    outer = lax.dot_general(flat, delta[...], TN, preferred_element_type=F32)
    pairs = []
    for which in range(3):
        top = outer[which * 128 : which * 128 + 64]
        low = outer[which * 128 + 64 : which * 128 + 128]
        pairs.append((top + pltpu.roll(low, 64, 1), pltpu.roll(top, 64, 1) + low))
    return pairs


def backward1_body(total, tgt, px, q, states, xsum, rl, wb, sinv, rinv, lik, direct, usta, usrc, hi, lo, rgt, lft, wpart, delta):
    rows, cols, _ = q.shape
    sums = jnp.sum(total[...], axis=0)
    counts = pltpu.roll(sums, 64, 1)[:, :cols]
    logits = sums[:, :cols] / jnp.sqrt(jnp.maximum(counts, 1.0))
    lik[...] = logits[:2, :]
    error = jax.nn.sigmoid(logits) - tgt[...]
    error = jnp.concatenate([error, jnp.zeros((8, cols), F32)], 0).astype(BF)
    unit = onehot(iota((cols, cols), 0) == iota((cols, cols), 1))
    choose = onehot((iota((16, 128), 1) >> 6) == iota((16, 128), 0))
    wide = dot(dot_nt(unit, error).astype(BF), choose)
    read = rl[0:1, :]

    def make(p):
        score = px[8 * p : 8 * p + 8].astype(F32) * wide[None]
        return score.reshape(8 * cols, 128) * read

    pairs = backward_tail(make, q, states, wb, sinv, rinv, 1, delta, direct, usta, usrc, (hi, lo, rgt, lft))
    lane = iota((64, 128), 1) < 64
    wpart[0:64, :] = jnp.where(lane, pairs[0][0], pairs[1][1])
    wpart[64:128, :] = pairs[2][0]
    v = jnp.sum(wide * xsum[...], axis=0, keepdims=True)
    v = jnp.broadcast_to(v, (8, 128))
    wpart[128:136, :] = v + pltpu.roll(v, 64, 1)


def gathered(direct, usta, usrc, up, down, left, right, tk, qk, hold):
    rows, cols, _ = direct.shape
    for g, part in enumerate(mix_sta(tk, up, usta, down)):
        hold[:, g * HW : (g + 1) * HW, :] = part.reshape(rows, HW, 128)

    def make(p):
        cut = slice(8 * p, 8 * p + 8)
        base = (direct[cut] + hold[cut]).reshape(8 * cols, 128)
        return base + mix_src(qk, left, usrc, right, 8 * p)

    return make


def backward0_body(direct1, usta1, usrc1, up, down, left, right, tk, qk, q, states, wb, sinv, rinv, wpart, direct, usta, usrc, hi, lo, rgt, lft, pay, delta, hold):
    make = gathered(direct1, usta1, usrc1, up, down, left, right, tk, qk, hold)
    pairs = backward_tail(make, q, states, wb, sinv, rinv, 0, delta, direct, usta, usrc, (hi, lo, rgt, lft))
    lane = iota((64, 128), 1) < 64
    pay[0:64, :] = wpart[0:64, :]
    pay[64:128, :] = jnp.where(lane, wpart[64:128, :], pairs[2][1])
    pay[128:192, :] = jnp.where(lane, pairs[0][0], pairs[1][1])
    pay[192:200, :] = wpart[128:136, :]
    pay[200:, :] = jnp.zeros((pay.shape[0] - 200, 128), F32)


def last_body(direct, usta, usrc, up, down, left, right, tk, qk, out, hold):
    make = gathered(direct, usta, usrc, up, down, left, right, tk, qk, hold)
    cols = direct.shape[1]
    for p in range(direct.shape[0] // 8):
        out[8 * p : 8 * p + 8] = make(p).astype(BF).reshape(8, cols, 128)


def sum_body(x, out):
    out[...] = jnp.broadcast_to(jnp.sum(x[...], axis=0)[None], out.shape)


def unpack_body(factor, x, w, v):
    flat = x[...].reshape(-1, 128) * factor
    first = flat[0:64]
    second = flat[64:128]
    third = flat[128:192]
    w[1, 0] = first[:, :64]
    w[1, 1] = pltpu.roll(first, 64, 1)[:, :64]
    w[1, 2] = second[:, :64]
    w[0, 2] = pltpu.roll(second, 64, 1)[:, :64]
    w[0, 0] = third[:, :64]
    w[0, 1] = pltpu.roll(third, 64, 1)[:, :64]
    v[...] = flat[192:193, :64]


def scratch_call(body, outs, scratch, *args):
    vm = pl.BlockSpec(memory_space=pltpu.VMEM)
    return pl.pallas_call(
        body,
        out_shape=[jax.ShapeDtypeStruct(s, d) for s, d in outs],
        in_specs=[vm] * len(args),
        out_specs=[vm] * len(outs),
        scratch_shapes=[pltpu.VMEM(s, d) for s, d in scratch],
        compiler_params=pltpu.CompilerParams(vmem_limit_bytes=VMEM_LIMIT),
    )(*args)


def halo(hi, lo, right, left):
    sta, src = lax.axis_size("sta"), lax.axis_size("z") * lax.axis_size("xh")
    ups = [(i, i + 1) for i in range(sta - 1)]
    rights = [(i, i + 1) for i in range(src - 1)]
    from_up = lax.ppermute(hi, "sta", ups)
    from_down = lax.ppermute(lo, "sta", [(b, a) for a, b in ups])
    from_left = lax.ppermute(right, SRC, rights)
    from_right = lax.ppermute(left, SRC, [(b, a) for a, b in rights])
    return from_up, from_down, from_left, from_right


def shards(features, station_lists, station_counts, source_lists, source_counts, picks, targets, layer_weights, readout_vector):
    rows, cols, channels = features.shape
    n_sta = lax.axis_size("sta")
    n_z = lax.axis_size("z")
    n_plane = n_sta * lax.axis_size("xh")
    whole = (rows, cols, channels)
    edge_outs = [((HW, cols, channels), BF)] * 2 + [((rows, HW, channels), BF)] * 2
    ext_sta, ext_src = rows + 2 * HW, cols + 2 * HW

    edges = call(edge_body, edge_outs, features)
    sk, tk, rk, qk, sinv, rinv, wf, wb, px, cnt, tgt, rl = call(
        lambda *refs: prep_body(rows, cols, *refs),
        [
            ((rows * HW, ext_sta * HW), BF),
            ((rows * HW, ext_sta * HW), BF),
            ((4 * cols, 4 * ext_src), BF),
            ((4 * cols, 4 * ext_src), BF),
            ((rows * HW, channels), F32),
            ((4 * cols, channels), F32),
            ((LAYERS, 3 * channels, channels), BF),
            ((LAYERS, channels, 3 * channels), BF),
            (whole, BF),
            ((8, channels), F32),
            ((8, cols), F32),
            ((8, channels), F32),
        ],
        station_lists,
        station_counts.reshape(1, -1),
        source_lists,
        source_counts.reshape(1, -1),
        picks,
        targets,
        layer_weights,
        readout_vector.reshape(1, -1),
    )
    state_outs = [((rows, cols, 3 * channels), BF), (whole, F32)]
    got = halo(*edges)
    h1, *edges, states0, q0 = call(
        forward0_body, [(whole, BF)] + edge_outs + state_outs, features, *got, sk, rk, sinv, rinv, wf
    )
    got = halo(*edges)
    states1, q1, xsum, block = call(
        forward1_body,
        state_outs + [((cols, channels), F32), ((n_sta, 8, channels), F32)],
        h1,
        *got,
        sk,
        rk,
        sinv,
        rinv,
        wf,
        px,
        cnt,
        rl,
    )
    total = lax.all_to_all(block, "sta", 0, 0)
    grad_outs = [(whole, F32), (whole, BF), (whole, BF)] + edge_outs
    flat = ((rows * cols, channels), BF)
    likelihood, direct, usta, usrc, *edges, wpart = scratch_call(
        backward1_body,
        [((2, cols), F32)] + grad_outs + [((136, channels), F32)],
        [flat],
        total,
        tgt,
        px,
        q1,
        states1,
        xsum,
        rl,
        wb,
        sinv,
        rinv,
    )
    got = halo(*edges)
    per = -(-200 // (8 * n_plane)) * 8
    direct, usta, usrc, *edges, pay = scratch_call(
        backward0_body,
        grad_outs + [((per * n_plane, channels), F32)],
        [flat, (whole, F32)],
        direct,
        usta,
        usrc,
        *got,
        tk,
        qk,
        q0,
        states0,
        wb,
        sinv,
        rinv,
        wpart,
    )
    got = halo(*edges)
    (feature_grad,) = scratch_call(last_body, [(whole, BF)], [(whole, F32)], direct, usta, usrc, *got, tk, qk)
    part = lax.all_to_all(pay.reshape(n_plane, per, channels), PLANE, 0, 0)
    (part,) = call(sum_body, [((n_z, per, channels), F32)], part)
    part = lax.all_to_all(part, "z", 0, 0)
    (part,) = call(sum_body, [((n_plane, per, channels), F32)], part)
    part = lax.all_to_all(part, PLANE, 0, 0)
    nodes = float(rows * n_sta * cols * lax.axis_size("z") * lax.axis_size("xh"))
    feature = layer_weights.shape[-1]
    weight_grad, vector_grad = call(
        lambda *refs: unpack_body(nodes**-0.5, *refs),
        [(layer_weights.shape, F32), ((1, feature), F32)],
        part,
    )
    return likelihood, feature_grad, weight_grad, vector_grad.reshape(feature)


def solution(mesh):
    n_sta, n_src = mesh.devices.shape
    near = 2
    fine = Mesh(mesh.devices.reshape(n_sta, n_src // near, near), ("sta",) + SRC)
    in_specs = (P("sta", SRC, None), P(), P(), P(), P(), P(None, "sta"), P(None, SRC), P(), P())
    out_specs = (P(None, SRC), P("sta", SRC, None), P(), P())
    return jax.shard_map(shards, mesh=fine, in_specs=in_specs, out_specs=out_specs, check_vma=False)
```

```python
import jax
import jax.numpy as jnp
from jax import lax
from jax.experimental import pallas as pl
from jax.experimental.pallas import tpu as pltpu
from jax.sharding import Mesh
from jax.sharding import PartitionSpec as P

LAYERS = 2
HW = 16
BF = jnp.bfloat16
F32 = jnp.float32
PLANE = ("sta", "xh")
SRC = ("z", "xh")
NT = (((1,), (1,)), ((), ()))
TN = (((0,), (0,)), ((), ()))
VMEM_LIMIT = 40 * 1024 * 1024


def iota(shape, dim):
    return lax.broadcasted_iota(jnp.int32, shape, dim)


def dot(a, b):
    return jnp.dot(a, b, preferred_element_type=F32)


def dot_nt(a, b, precision=None):
    return lax.dot_general(a, b, NT, precision=precision, preferred_element_type=F32)


def onehot(mask):
    return jnp.where(mask, 1.0, 0.0).astype(BF)


def call(body, outs, *args):
    vm = pl.BlockSpec(memory_space=pltpu.VMEM)
    return pl.pallas_call(
        body,
        out_shape=[jax.ShapeDtypeStruct(s, d) for s, d in outs],
        in_specs=[vm] * len(args),
        out_specs=[vm] * len(outs),
        compiler_params=pltpu.CompilerParams(vmem_limit_bytes=VMEM_LIMIT),
    )(*args)


def count_rows(counts_ref, first, rows):
    total = counts_ref.shape[1]
    hit = onehot(iota((rows, total), 1) == iota((rows, total), 0) + first)
    every = jnp.broadcast_to(counts_ref[...].astype(F32), (128, total)).astype(BF)
    return dot_nt(hit, every)


def list_counts(lists, counts, first, span):
    rows = lists.shape[0]
    shifted = lists - first
    cols = iota((rows, span), 1)
    acc = jnp.zeros((rows, span), F32)
    for k in range(lists.shape[1]):
        hit = (shifted[:, k : k + 1] == cols) & (counts[:, :span] > k)
        acc = acc + jnp.where(hit, 1.0, 0.0)
    return acc.astype(BF)


def mixes(lists_ref, counts_ref, first, own):
    total = lists_ref.shape[0]
    lo = pl.multiple_of(jnp.maximum(first - HW, 0), HW)
    mid = pl.multiple_of(first, HW)
    hi = pl.multiple_of(jnp.minimum(first + own, total - HW), HW)
    mine = lists_ref[pl.ds(mid, own), :]
    wide = jnp.concatenate([lists_ref[pl.ds(lo, HW), :], mine, lists_ref[pl.ds(hi, HW), :]], 0)
    own_counts = count_rows(counts_ref, first, own)
    wide_counts = count_rows(counts_ref, first - HW, own + 2 * HW)
    span = own + 2 * HW
    gather = list_counts(mine, own_counts, first - HW, span)
    scatter = list_counts(wide, wide_counts, first, own)
    return gather, scatter, own_counts


def prep_body(sta_rows, src_rows, *refs):
    (slists, scounts, rlists, rcounts, picks, targets, weights, readout) = refs[:8]
    (sk, tk, rk, qk, sinv, rinv, wf, wb, px, cnt, tgt, rl) = refs[8:]
    sta_first = lax.axis_index("sta") * sta_rows
    src_first = (lax.axis_index("z") * lax.axis_size("xh") + lax.axis_index("xh")) * src_rows
    feature = weights.shape[-1]
    channels = 2 * feature

    gather, scatter, own_counts = mixes(slists, scounts, sta_first, sta_rows)
    ext = sta_rows + 2 * HW
    spread_cols = onehot(iota((ext, ext * HW), 1) >> 4 == iota((ext, ext * HW), 0))
    step = 128
    per = step // HW
    lane_mask = (iota((step, ext * HW), 0) & 15) == (iota((step, ext * HW), 1) & 15)
    for part in range(sta_rows * HW // step):
        pick_rows = onehot((iota((step, sta_rows), 0) >> 4) + part * per == iota((step, sta_rows), 1))
        for source, target, form in ((gather, sk, dot), (scatter, tk, dot_nt)):
            rows = form(pick_rows, source).astype(BF)
            full = dot(rows, spread_cols)
            target[part * step : (part + 1) * step, :] = jnp.where(lane_mask, full, 0.0).astype(BF)
        inverse = 1.0 / dot(pick_rows, own_counts.astype(BF))
        sinv[part * step : (part + 1) * step, :] = inverse

    gather, scatter, own_counts = mixes(rlists, rcounts, src_first, src_rows)
    ext = src_rows + 2 * HW
    rows_n, cols_n = 4 * src_rows, 4 * ext
    pick_rows = onehot((iota((rows_n, src_rows), 0) & (src_rows - 1)) == iota((rows_n, src_rows), 1))
    spread_cols = onehot((iota((ext, cols_n), 1) & (ext - 1)) == iota((ext, cols_n), 0))
    block_mask = (iota((rows_n, cols_n), 0) >> 5) == (iota((rows_n, cols_n), 1) >> 6)
    for source, target, form in ((gather, rk, dot), (scatter, qk, dot_nt)):
        full = dot(form(pick_rows, source).astype(BF), spread_cols)
        target[...] = jnp.where(block_mask, full, 0.0).astype(BF)
    rinv[...] = 1.0 / dot(pick_rows, own_counts.astype(BF))

    twice = onehot((iota((feature, channels), 1) & (feature - 1)) == iota((feature, channels), 0))
    unit = onehot(iota((feature, feature), 0) == iota((feature, feature), 1))
    left = iota((feature, channels), 1) < feature
    for layer in range(LAYERS):
        for which in range(3):
            matrix = weights[layer, which]
            plain = dot(matrix, twice)
            turned = dot_nt(unit, jnp.concatenate([matrix, matrix], 0))
            at = which * channels
            wf[layer, at : at + feature, :] = jnp.where(left, plain, 0.0).astype(BF)
            wf[layer, at + feature : at + channels, :] = jnp.where(left, 0.0, plain).astype(BF)
            wb[layer, :feature, at : at + channels] = jnp.where(left, turned, 0.0).astype(BF)
            wb[layer, feature:, at : at + channels] = jnp.where(left, 0.0, turned).astype(BF)
    rl[...] = dot(jnp.broadcast_to(readout[...].astype(F32), (16, feature)).astype(BF), twice)[:8]

    window = iota((16, sta_rows), 0)
    picked = picks[...].astype(F32)
    rows = jnp.where(window == 0, picked[0:1, :], jnp.where(window == 1, picked[1:2, :], 0.0)).astype(BF)
    choose = onehot((iota((16, channels), 1) >> 6) == iota((16, channels), 0))
    chunk = 256
    for part in range(sta_rows * src_rows // chunk):
        at = part * chunk
        own = onehot((iota((chunk, sta_rows), 0) + at) >> 5 == iota((chunk, sta_rows), 1))
        wide = dot(dot_nt(own, rows).astype(BF), choose).astype(BF)
        span = chunk // src_rows
        px[part * span : (part + 1) * span] = wide.reshape(span, src_rows, channels)
    cnt[...] = dot(rows, jnp.ones((sta_rows, channels), BF))[:8]
    line = iota((8, src_rows), 0)
    aims = targets[...]
    tgt[...] = jnp.where(line == 0, aims[0:1, :], jnp.where(line == 1, aims[1:2, :], 0.0))


def edge_body(x, hi, lo, right, left):
    store_edges(x, x, hi, lo, right, left)


def store_edges(rows, cols, hi, lo, right, left):
    hi[...] = rows[rows.shape[0] - HW :]
    lo[...] = rows[:HW]
    right[...] = cols[:, cols.shape[1] - HW :]
    left[...] = cols[:, :HW]


def mix_sta(mix, up, own, down):
    span = own.shape[0] + 2 * HW
    parts = []
    for g in range(own.shape[1] // HW):
        cut = slice(g * HW, (g + 1) * HW)
        parts.append(
            jnp.concatenate([up[:, cut], own[:, cut], down[:, cut]], 0).reshape(span * HW, 128)
        )
    out = dot(mix[...], jnp.concatenate(parts, 1))
    return [out[:, g * 128 : (g + 1) * 128] for g in range(len(parts))]


def mix_src(mix, left, own, right, first):
    parts = []
    for at in (first, first + 4):
        cut = slice(at, at + 4)
        joined = jnp.concatenate([left[cut], own[cut], right[cut]], 1)
        parts.append(joined.reshape(4 * joined.shape[1], 128))
    out = dot(mix[...], jnp.concatenate(parts, 1))
    return jnp.concatenate([out[:, :128], out[:, 128:]], 0)


def forward_parts(h, up, down, left, right, sk, rk, sinv, rinv, wf, states, keep, layer):
    rows, cols, _ = h.shape
    for g, part in enumerate(mix_sta(sk, up, h, down)):
        mean = (part * sinv[...]).astype(BF).reshape(rows, HW, 128)
        states[:, g * HW : (g + 1) * HW, 128:256] = mean
    states[:, :, :128] = h[...]
    both = jnp.concatenate([rinv[...], rinv[...]], 0)
    for p in range(rows // 8):
        cut = slice(8 * p, 8 * p + 8)
        mean = (mix_src(rk, left, h, right, 8 * p) * both).astype(BF)
        states[cut, :, 256:384] = mean.reshape(8, cols, 128)
        z = dot(states[cut].reshape(8 * cols, 384), wf[layer])
        t = jnp.tanh(z)
        keep[cut] = (1.0 - t * t).reshape(8, cols, 128)
        before = h[cut].reshape(8 * cols, 128).astype(F32)
        yield cut, (before + t).astype(BF)


def forward0_body(h, left, right, up, down, sk, rk, sinv, rinv, wf, nxt, hi, lo, rgt, lft, states, keep):
    cols = h.shape[1]
    for cut, after in forward_parts(h, up, down, left, right, sk, rk, sinv, rinv, wf, states, keep, 0):
        nxt[cut] = after.reshape(8, cols, 128)
    store_edges(nxt, nxt, hi, lo, rgt, lft)


def forward1_body(h, left, right, up, down, sk, rk, sinv, rinv, wf, px, cnt, rl, states, keep, xsum, block):
    cols = h.shape[1]
    acc = jnp.zeros((cols, 128), F32)
    for cut, after in forward_parts(h, up, down, left, right, sk, rk, sinv, rinv, wf, states, keep, 1):
        part = after.astype(F32).reshape(8, cols, 128) * px[cut].astype(F32)
        acc = acc + jnp.sum(part, axis=0)
    xsum[...] = acc
    read = jnp.where((iota((8, 128), 1) >> 6) == iota((8, 128), 0), rl[...], 0.0)
    padded = jnp.concatenate([acc, jnp.zeros((128 - cols, 128), F32)], 0)
    sums = dot_nt(read, padded, precision=lax.Precision.HIGHEST)
    mixed = jnp.where(iota((8, 128), 1) < 64, sums, cnt[...])
    block[...] = jnp.broadcast_to(mixed[None], block.shape)


def backward_tail(make, q, states, wb, sinv, rinv, layer, delta, direct, usta, usrc, edges):
    rows, cols, _ = q.shape
    both = jnp.concatenate([rinv[...], rinv[...]], 0)
    for p in range(rows // 8):
        cut = slice(8 * p, 8 * p + 8)
        grad = make(p)
        d = (grad * q[cut].reshape(8 * cols, 128)).astype(BF)
        delta[8 * cols * p : 8 * cols * (p + 1), :] = d
        u = dot(d, wb[layer])
        direct[cut] = (grad + u[:, :128]).reshape(8, cols, 128)
        scale = sinv[8 * HW * p : 8 * HW * (p + 1), :].reshape(8, HW, 128)
        scale = jnp.concatenate([scale] * (cols // HW), 1)
        usta[cut] = (u[:, 128:256].reshape(8, cols, 128) * scale).astype(BF)
        usrc[cut] = (u[:, 256:384] * both).astype(BF).reshape(8, cols, 128)
    store_edges(usta, usrc, *edges)
    flat = states[...].reshape(rows * cols, 384)
    outer = lax.dot_general(flat, delta[...], TN, preferred_element_type=F32)
    pairs = []
    for which in range(3):
        top = outer[which * 128 : which * 128 + 64]
        low = outer[which * 128 + 64 : which * 128 + 128]
        pairs.append((top + pltpu.roll(low, 64, 1), pltpu.roll(top, 64, 1) + low))
    return pairs


def backward1_body(total, tgt, px, q, states, xsum, rl, wb, sinv, rinv, lik, direct, usta, usrc, hi, lo, rgt, lft, wpart, delta):
    rows, cols, _ = q.shape
    sums = jnp.sum(total[...], axis=0)
    counts = pltpu.roll(sums, 64, 1)[:, :cols]
    logits = sums[:, :cols] / jnp.sqrt(jnp.maximum(counts, 1.0))
    lik[...] = logits[:2, :]
    error = jax.nn.sigmoid(logits) - tgt[...]
    error = jnp.concatenate([error, jnp.zeros((8, cols), F32)], 0).astype(BF)
    unit = onehot(iota((cols, cols), 0) == iota((cols, cols), 1))
    choose = onehot((iota((16, 128), 1) >> 6) == iota((16, 128), 0))
    wide = dot(dot_nt(unit, error).astype(BF), choose)
    read = rl[0:1, :]

    def make(p):
        score = px[8 * p : 8 * p + 8].astype(F32) * wide[None]
        return score.reshape(8 * cols, 128) * read

    pairs = backward_tail(make, q, states, wb, sinv, rinv, 1, delta, direct, usta, usrc, (hi, lo, rgt, lft))
    lane = iota((64, 128), 1) < 64
    wpart[0:64, :] = jnp.where(lane, pairs[0][0], pairs[1][1])
    wpart[64:128, :] = pairs[2][0]
    v = jnp.sum(wide * xsum[...], axis=0, keepdims=True)
    v = jnp.broadcast_to(v, (8, 128))
    wpart[128:136, :] = v + pltpu.roll(v, 64, 1)


def gathered(direct, usta, usrc, up, down, left, right, tk, qk, hold):
    rows, cols, _ = direct.shape
    for g, part in enumerate(mix_sta(tk, up, usta, down)):
        hold[:, g * HW : (g + 1) * HW, :] = part.reshape(rows, HW, 128)

    def make(p):
        cut = slice(8 * p, 8 * p + 8)
        base = (direct[cut] + hold[cut]).reshape(8 * cols, 128)
        return base + mix_src(qk, left, usrc, right, 8 * p)

    return make


def backward0_body(direct1, usta1, usrc1, left, right, up, down, tk, qk, q, states, wb, sinv, rinv, wpart, direct, usta, usrc, hi, lo, rgt, lft, pay, delta, hold):
    make = gathered(direct1, usta1, usrc1, up, down, left, right, tk, qk, hold)
    pairs = backward_tail(make, q, states, wb, sinv, rinv, 0, delta, direct, usta, usrc, (hi, lo, rgt, lft))
    lane = iota((64, 128), 1) < 64
    pay[0:64, :] = wpart[0:64, :]
    pay[64:128, :] = jnp.where(lane, wpart[64:128, :], pairs[2][1])
    pay[128:192, :] = jnp.where(lane, pairs[0][0], pairs[1][1])
    pay[192:200, :] = wpart[128:136, :]
    pay[200:, :] = jnp.zeros((pay.shape[0] - 200, 128), F32)


def last_body(direct, usta, usrc, left, right, up, down, tk, qk, out, hold):
    make = gathered(direct, usta, usrc, up, down, left, right, tk, qk, hold)
    cols = direct.shape[1]
    for p in range(direct.shape[0] // 8):
        out[8 * p : 8 * p + 8] = make(p).astype(BF).reshape(8, cols, 128)


def sum_body(x, out):
    out[...] = jnp.broadcast_to(jnp.sum(x[...], axis=0)[None], out.shape)


def unpack_body(factor, x, w, v):
    flat = x[...].reshape(-1, 128) * factor
    first = flat[0:64]
    second = flat[64:128]
    third = flat[128:192]
    w[1, 0] = first[:, :64]
    w[1, 1] = pltpu.roll(first, 64, 1)[:, :64]
    w[1, 2] = second[:, :64]
    w[0, 2] = pltpu.roll(second, 64, 1)[:, :64]
    w[0, 0] = third[:, :64]
    w[0, 1] = pltpu.roll(third, 64, 1)[:, :64]
    v[...] = flat[192:193, :64]


def scratch_call(body, outs, scratch, *args):
    vm = pl.BlockSpec(memory_space=pltpu.VMEM)
    return pl.pallas_call(
        body,
        out_shape=[jax.ShapeDtypeStruct(s, d) for s, d in outs],
        in_specs=[vm] * len(args),
        out_specs=[vm] * len(outs),
        scratch_shapes=[pltpu.VMEM(s, d) for s, d in scratch],
        compiler_params=pltpu.CompilerParams(vmem_limit_bytes=VMEM_LIMIT),
    )(*args)


def shifts(axis):
    count = 1
    for name in axis if isinstance(axis, tuple) else (axis,):
        count *= lax.axis_size(name)
    ups = [(i, i + 1) for i in range(count - 1)]
    return ups, [(b, a) for a, b in ups]


def trade(high, low, axis):
    ups, downs = shifts(axis)
    return lax.ppermute(high, axis, ups), lax.ppermute(low, axis, downs)


def halo(hi, lo, right, left):
    from_left, from_right = trade(right, left, SRC)
    from_up, from_down = trade(hi, lo, "sta")
    return from_left, from_right, from_up, from_down


def shards(features, station_lists, station_counts, source_lists, source_counts, picks, targets, layer_weights, readout_vector):
    rows, cols, channels = features.shape
    n_sta = lax.axis_size("sta")
    n_z = lax.axis_size("z")
    n_plane = n_sta * lax.axis_size("xh")
    whole = (rows, cols, channels)
    edge_outs = [((HW, cols, channels), BF)] * 2 + [((rows, HW, channels), BF)] * 2
    ext_sta, ext_src = rows + 2 * HW, cols + 2 * HW

    edges = call(edge_body, edge_outs, features)
    sk, tk, rk, qk, sinv, rinv, wf, wb, px, cnt, tgt, rl = call(
        lambda *refs: prep_body(rows, cols, *refs),
        [
            ((rows * HW, ext_sta * HW), BF),
            ((rows * HW, ext_sta * HW), BF),
            ((4 * cols, 4 * ext_src), BF),
            ((4 * cols, 4 * ext_src), BF),
            ((rows * HW, channels), F32),
            ((4 * cols, channels), F32),
            ((LAYERS, 3 * channels, channels), BF),
            ((LAYERS, channels, 3 * channels), BF),
            (whole, BF),
            ((8, channels), F32),
            ((8, cols), F32),
            ((8, channels), F32),
        ],
        station_lists,
        station_counts.reshape(1, -1),
        source_lists,
        source_counts.reshape(1, -1),
        picks,
        targets,
        layer_weights,
        readout_vector.reshape(1, -1),
    )
    state_outs = [((rows, cols, 3 * channels), BF), (whole, F32)]
    got = halo(*edges)
    h1, *edges, states0, q0 = call(
        forward0_body, [(whole, BF)] + edge_outs + state_outs, features, *got, sk, rk, sinv, rinv, wf
    )
    got = halo(*edges)
    states1, q1, xsum, block = call(
        forward1_body,
        state_outs + [((cols, channels), F32), ((n_sta, 8, channels), F32)],
        h1,
        *got,
        sk,
        rk,
        sinv,
        rinv,
        wf,
        px,
        cnt,
        rl,
    )
    total = lax.all_to_all(block, "sta", 0, 0)
    grad_outs = [(whole, F32), (whole, BF), (whole, BF)] + edge_outs
    flat = ((rows * cols, channels), BF)
    likelihood, direct, usta, usrc, *edges, wpart = scratch_call(
        backward1_body,
        [((2, cols), F32)] + grad_outs + [((136, channels), F32)],
        [flat],
        total,
        tgt,
        px,
        q1,
        states1,
        xsum,
        rl,
        wb,
        sinv,
        rinv,
    )
    got = halo(*edges)
    per = -(-200 // (8 * n_plane)) * 8
    direct, usta, usrc, *edges, pay = scratch_call(
        backward0_body,
        grad_outs + [((per * n_plane, channels), F32)],
        [flat, (whole, F32)],
        direct,
        usta,
        usrc,
        *got,
        tk,
        qk,
        q0,
        states0,
        wb,
        sinv,
        rinv,
        wpart,
    )
    hi, lo, right, left = edges
    from_left, from_right = trade(right, left, SRC)
    part = lax.all_to_all(pay.reshape(n_plane, per, channels), PLANE, 0, 0)
    part, from_left, from_right, hi, lo = lax.optimization_barrier((part, from_left, from_right, hi, lo))
    (part,) = call(sum_body, [((n_z, per, channels), F32)], part)
    part = lax.all_to_all(part, "z", 0, 0)
    from_up, from_down = trade(hi, lo, "sta")
    part, from_up, from_down = lax.optimization_barrier((part, from_up, from_down))
    (part,) = call(sum_body, [((n_plane, per, channels), F32)], part)
    part = lax.all_to_all(part, PLANE, 0, 0)
    (feature_grad,) = scratch_call(
        last_body,
        [(whole, BF)],
        [(whole, F32)],
        direct,
        usta,
        usrc,
        from_left,
        from_right,
        from_up,
        from_down,
        tk,
        qk,
    )
    nodes = float(rows * n_sta * cols * lax.axis_size("z") * lax.axis_size("xh"))
    feature = layer_weights.shape[-1]
    weight_grad, vector_grad = call(
        lambda *refs: unpack_body(nodes**-0.5, *refs),
        [(layer_weights.shape, F32), ((1, feature), F32)],
        part,
    )
    return likelihood, feature_grad, weight_grad, vector_grad.reshape(feature)


def solution(mesh):
    n_sta, n_src = mesh.devices.shape
    near = 2
    fine = Mesh(mesh.devices.reshape(n_sta, n_src // near, near), ("sta",) + SRC)
    in_specs = (P("sta", SRC, None), P(), P(), P(), P(), P(None, "sta"), P(None, SRC), P(), P())
    out_specs = (P(None, SRC), P("sta", SRC, None), P(), P())
    return jax.shard_map(shards, mesh=fine, in_specs=in_specs, out_specs=out_specs, check_vma=False)
```

```python
import jax
import jax.numpy as jnp
from jax import lax
from jax.experimental import pallas as pl
from jax.experimental.pallas import tpu as pltpu
from jax.sharding import Mesh
from jax.sharding import PartitionSpec as P

LAYERS = 2
HW = 16
BF = jnp.bfloat16
F32 = jnp.float32
PLANE = ("sta", "xh")
SRC = ("z", "xh")
NT = (((1,), (1,)), ((), ()))
TN = (((0,), (0,)), ((), ()))
VMEM_LIMIT = 16 * 1024 * 1024


def iota(shape, dim):
    return lax.broadcasted_iota(jnp.int32, shape, dim)


def dot(a, b):
    return jnp.dot(a, b, preferred_element_type=F32)


def dot_nt(a, b, precision=None):
    return lax.dot_general(a, b, NT, precision=precision, preferred_element_type=F32)


def onehot(mask):
    return jnp.where(mask, 1.0, 0.0).astype(BF)


def call(body, outs, *args):
    vm = pl.BlockSpec(memory_space=pltpu.VMEM)
    return pl.pallas_call(
        body,
        out_shape=[jax.ShapeDtypeStruct(s, d) for s, d in outs],
        in_specs=[vm] * len(args),
        out_specs=[vm] * len(outs),
        compiler_params=pltpu.CompilerParams(vmem_limit_bytes=VMEM_LIMIT),
    )(*args)


def even(axis):
    at = jnp.int32(0)
    for name in axis if isinstance(axis, tuple) else (axis,):
        at = at * lax.axis_size(name) + lax.axis_index(name)
    return (at & 1) == 0, at


def offsets(spot, own, flag):
    jump = own + HW
    first = jnp.where(flag, spot, spot - jump)
    second = jnp.where(flag, spot - HW - jump, spot - HW)
    return jnp.where(spot < own, spot, jnp.where(spot < own + HW, first, second))


def count_rows(counts_ref, first, rows, own, flag):
    total = counts_ref.shape[1]
    hit = onehot(iota((rows, total), 1) == offsets(iota((rows, total), 0), own, flag) + first)
    every = jnp.broadcast_to(counts_ref[...].astype(F32), (128, total)).astype(BF)
    return dot_nt(hit, every)


def list_counts(lists, counts, first, places):
    span = places.shape[1]
    shifted = lists - first
    acc = jnp.zeros(places.shape, F32)
    for k in range(lists.shape[1]):
        hit = (shifted[:, k : k + 1] == places) & (counts[:, :span] > k)
        acc = acc + jnp.where(hit, 1.0, 0.0)
    return acc.astype(BF)


def gather_counts(lists_ref, counts_ref, first, own, flag):
    span = own + 2 * HW
    mine = lists_ref[pl.ds(pl.multiple_of(first, HW), own), :]
    counts = count_rows(counts_ref, first, own, own, flag)
    return list_counts(mine, counts, first, offsets(iota((own, span), 1), own, flag)), counts


def scatter_counts(lists_ref, counts_ref, first, own, flag):
    total = lists_ref.shape[0]
    above = jnp.maximum(first - HW, 0)
    below = jnp.minimum(first + own, total - HW)
    parts = [lists_ref[pl.ds(pl.multiple_of(first, HW), own), :]]
    for start in (jnp.where(flag, below, above), jnp.where(flag, above, below)):
        parts.append(lists_ref[pl.ds(pl.multiple_of(start, HW), HW), :])
    counts = count_rows(counts_ref, first, own + 2 * HW, own, flag)
    return list_counts(jnp.concatenate(parts, 0), counts, first, iota((own + 2 * HW, own), 1))


def wide_sta(mix, target, form, own):
    ext = own + 2 * HW
    step = 128
    per = step // HW
    spread_cols = onehot(iota((ext, ext * HW), 1) >> 4 == iota((ext, ext * HW), 0))
    lane_mask = (iota((step, ext * HW), 0) & 15) == (iota((step, ext * HW), 1) & 15)
    for part in range(own * HW // step):
        pick_rows = onehot((iota((step, own), 0) >> 4) + part * per == iota((step, own), 1))
        full = dot(form(pick_rows, mix).astype(BF), spread_cols)
        target[part * step : (part + 1) * step, :] = jnp.where(lane_mask, full, 0.0).astype(BF)


def src_picks(own):
    return onehot((iota((4 * own, own), 0) & (own - 1)) == iota((4 * own, own), 1))


def wide_src(mix, target, form, own):
    ext = own + 2 * HW
    spread_cols = onehot((iota((ext, 4 * ext), 1) & (ext - 1)) == iota((ext, 4 * ext), 0))
    block_mask = (iota((4 * own, 4 * ext), 0) >> 5) == (iota((4 * own, 4 * ext), 1) >> 6)
    full = dot(form(src_picks(own), mix).astype(BF), spread_cols)
    target[...] = jnp.where(block_mask, full, 0.0).astype(BF)


def doubling(feature):
    channels = 2 * feature
    return onehot((iota((feature, channels), 1) & (feature - 1)) == iota((feature, channels), 0))


def prep0_body(sta_rows, src_rows, slists, scounts, rlists, rcounts, weights, sk, rk, sinv, rinv, wf):
    flag, at = even("sta")
    gather, counts = gather_counts(slists, scounts, at * sta_rows, sta_rows, flag)
    wide_sta(gather, sk, dot, sta_rows)
    pick_rows = onehot((iota((sta_rows * HW, sta_rows), 0) >> 4) == iota((sta_rows * HW, sta_rows), 1))
    sinv[...] = 1.0 / dot(pick_rows, counts.astype(BF))
    flag, at = even(SRC)
    gather, counts = gather_counts(rlists, rcounts, at * src_rows, src_rows, flag)
    wide_src(gather, rk, dot, src_rows)
    rinv[...] = 1.0 / dot(src_picks(src_rows), counts.astype(BF))
    feature = weights.shape[-1]
    channels = 2 * feature
    twice = doubling(feature)
    left = iota((feature, channels), 1) < feature
    for layer in range(LAYERS):
        for which in range(3):
            plain = dot(weights[layer, which], twice)
            at = which * channels
            wf[layer, at : at + feature, :] = jnp.where(left, plain, 0.0).astype(BF)
            wf[layer, at + feature : at + channels, :] = jnp.where(left, 0.0, plain).astype(BF)


def prep1_body(sta_rows, src_rows, *refs):
    (_, slists, scounts, rlists, rcounts, picks, targets, weights, readout) = refs[:9]
    (tk, qk, wb, px, cnt, tgt, rl) = refs[9:]
    flag, at = even("sta")
    wide_sta(scatter_counts(slists, scounts, at * sta_rows, sta_rows, flag), tk, dot_nt, sta_rows)
    flag, at = even(SRC)
    wide_src(scatter_counts(rlists, rcounts, at * src_rows, src_rows, flag), qk, dot_nt, src_rows)
    feature = weights.shape[-1]
    channels = 2 * feature
    unit = onehot(iota((feature, feature), 0) == iota((feature, feature), 1))
    left = iota((feature, channels), 1) < feature
    for layer in range(LAYERS):
        for which in range(3):
            matrix = weights[layer, which]
            turned = dot_nt(unit, jnp.concatenate([matrix, matrix], 0))
            at = which * channels
            wb[layer, :feature, at : at + channels] = jnp.where(left, turned, 0.0).astype(BF)
            wb[layer, feature:, at : at + channels] = jnp.where(left, 0.0, turned).astype(BF)
    twice = doubling(feature)
    rl[...] = dot(jnp.broadcast_to(readout[...].astype(F32), (16, feature)).astype(BF), twice)[:8]

    window = iota((16, sta_rows), 0)
    picked = picks[...].astype(F32)
    rows = jnp.where(window == 0, picked[0:1, :], jnp.where(window == 1, picked[1:2, :], 0.0)).astype(BF)
    choose = onehot((iota((16, channels), 1) >> 6) == iota((16, channels), 0))
    chunk = 256
    for part in range(sta_rows * src_rows // chunk):
        at = part * chunk
        own = onehot((iota((chunk, sta_rows), 0) + at) >> 5 == iota((chunk, sta_rows), 1))
        wide = dot(dot_nt(own, rows).astype(BF), choose).astype(BF)
        span = chunk // src_rows
        px[part * span : (part + 1) * span] = wide.reshape(span, src_rows, channels)
    cnt[...] = dot(rows, jnp.ones((sta_rows, channels), BF))[:8]
    line = iota((8, src_rows), 0)
    aims = targets[...]
    tgt[...] = jnp.where(line == 0, aims[0:1, :], jnp.where(line == 1, aims[1:2, :], 0.0))


def starts(axis, own):
    flag, _ = even(axis)
    last = jnp.int32(own - HW)
    none = jnp.int32(0)
    return [pl.multiple_of(jnp.where(f, last, none), HW) for f in (flag, jnp.logical_not(flag))]


def edge_body(x, c1, c0, r1, r0, sems):
    rows, cols, _ = x.shape
    s0, s1 = starts(SRC, cols)
    t0, t1 = starts("sta", rows)
    copies = [
        pltpu.make_async_copy(x.at[:, pl.ds(s1, HW)], c1, sems.at[0]),
        pltpu.make_async_copy(x.at[:, pl.ds(s0, HW)], c0, sems.at[1]),
        pltpu.make_async_copy(x.at[pl.ds(t1, HW)], r1, sems.at[2]),
        pltpu.make_async_copy(x.at[pl.ds(t0, HW)], r0, sems.at[3]),
    ]
    for copy in copies:
        copy.start()
    for copy in copies:
        copy.wait()


def store_edges(by_row, by_col, c1, c0, r1, r0):
    s0, s1 = starts(SRC, by_col.shape[1])
    t0, t1 = starts("sta", by_row.shape[0])
    c1[...] = by_col[:, pl.ds(s1, HW)]
    c0[...] = by_col[:, pl.ds(s0, HW)]
    r1[...] = by_row[pl.ds(t1, HW)]
    r0[...] = by_row[pl.ds(t0, HW)]


def mix_sta(mix, own, r0, r1):
    span = own.shape[0] + 2 * HW
    parts = []
    for g in range(own.shape[1] // HW):
        cut = slice(g * HW, (g + 1) * HW)
        parts.append(jnp.concatenate([own[:, cut], r0[:, cut], r1[:, cut]], 0).reshape(span * HW, 128))
    out = dot(mix[...], jnp.concatenate(parts, 1))
    return [out[:, g * 128 : (g + 1) * 128] for g in range(len(parts))]


def mix_src(mix, own, c0, c1, first):
    parts = []
    for at in (first, first + 4):
        cut = slice(at, at + 4)
        joined = jnp.concatenate([own[cut], c0[cut], c1[cut]], 1)
        parts.append(joined.reshape(4 * joined.shape[1], 128))
    out = dot(mix[...], jnp.concatenate(parts, 1))
    return jnp.concatenate([out[:, :128], out[:, 128:]], 0)


def forward_parts(h, c1, r1, c0, r0, sk, rk, sinv, rinv, wf, states, keep, layer):
    rows, cols, _ = h.shape
    for g, part in enumerate(mix_sta(sk, h, r0, r1)):
        mean = (part * sinv[...]).astype(BF).reshape(rows, HW, 128)
        states[:, g * HW : (g + 1) * HW, 128:256] = mean
    states[:, :, :128] = h[...]
    both = jnp.concatenate([rinv[...], rinv[...]], 0)
    for p in range(rows // 8):
        cut = slice(8 * p, 8 * p + 8)
        mean = (mix_src(rk, h, c0, c1, 8 * p) * both).astype(BF)
        states[cut, :, 256:384] = mean.reshape(8, cols, 128)
        z = dot(states[cut].reshape(8 * cols, 384), wf[layer])
        t = jnp.tanh(z)
        keep[cut] = (1.0 - t * t).reshape(8, cols, 128)
        before = h[cut].reshape(8 * cols, 128).astype(F32)
        yield cut, (before + t).astype(BF)


def forward0_body(h, c1, r1, c0, r0, sk, rk, sinv, rinv, wf, nxt, e1, e0, f1, f0, states, keep):
    cols = h.shape[1]
    for cut, after in forward_parts(h, c1, r1, c0, r0, sk, rk, sinv, rinv, wf, states, keep, 0):
        nxt[cut] = after.reshape(8, cols, 128)
    store_edges(nxt, nxt, e1, e0, f1, f0)


def forward1_body(h, c1, r1, c0, r0, sk, rk, sinv, rinv, wf, px, cnt, rl, states, keep, xsum, block):
    cols = h.shape[1]
    acc = jnp.zeros((cols, 128), F32)
    for cut, after in forward_parts(h, c1, r1, c0, r0, sk, rk, sinv, rinv, wf, states, keep, 1):
        part = after.astype(F32).reshape(8, cols, 128) * px[cut].astype(F32)
        acc = acc + jnp.sum(part, axis=0)
    xsum[...] = acc
    read = jnp.where((iota((8, 128), 1) >> 6) == iota((8, 128), 0), rl[...], 0.0)
    padded = jnp.concatenate([acc, jnp.zeros((128 - cols, 128), F32)], 0)
    sums = dot_nt(read, padded, precision=lax.Precision.HIGHEST)
    mixed = jnp.where(iota((8, 128), 1) < 64, sums, cnt[...])
    block[...] = jnp.broadcast_to(mixed[None], block.shape)


def send_back(p, grad, d, layer, wb, sinv, rinv, direct, usta, usrc):
    cols = usta.shape[1]
    cut = slice(8 * p, 8 * p + 8)
    both = jnp.concatenate([rinv[...], rinv[...]], 0)
    u = dot(d, wb[layer])
    direct[cut] = (grad + u[:, :128]).reshape(8, cols, 128)
    scale = sinv[8 * HW * p : 8 * HW * (p + 1), :].reshape(8, HW, 128)
    scale = jnp.concatenate([scale] * (cols // HW), 1)
    usta[cut] = (u[:, 128:256].reshape(8, cols, 128) * scale).astype(BF)
    usrc[cut] = (u[:, 256:384] * both).astype(BF).reshape(8, cols, 128)


def outer_pairs(states, delta):
    rows, cols, _ = states.shape
    flat = states[...].reshape(rows * cols, 384)
    outer = lax.dot_general(flat, delta[...], TN, preferred_element_type=F32)
    pairs = []
    for which in range(3):
        top = outer[which * 128 : which * 128 + 64]
        low = outer[which * 128 + 64 : which * 128 + 128]
        pairs.append((top + pltpu.roll(low, 64, 1), pltpu.roll(top, 64, 1) + low))
    return pairs


def backward1_body(total, tgt, px, q, rl, wb, sinv, rinv, lik, direct, usta, usrc, e1, e0, f1, f0, errs, delta):
    rows, cols, _ = q.shape
    sums = jnp.sum(total[...], axis=0)
    counts = pltpu.roll(sums, 64, 1)[:, :cols]
    logits = sums[:, :cols] / jnp.sqrt(jnp.maximum(counts, 1.0))
    lik[...] = logits[:2, :]
    error = jax.nn.sigmoid(logits) - tgt[...]
    error = jnp.concatenate([error, jnp.zeros((8, cols), F32)], 0).astype(BF)
    unit = onehot(iota((cols, cols), 0) == iota((cols, cols), 1))
    choose = onehot((iota((16, 128), 1) >> 6) == iota((16, 128), 0))
    wide = dot(dot_nt(unit, error).astype(BF), choose)
    errs[...] = wide
    read = rl[0:1, :]
    for p in range(rows // 8):
        cut = slice(8 * p, 8 * p + 8)
        score = px[cut].astype(F32) * wide[None]
        grad = score.reshape(8 * cols, 128) * read
        d = (grad * q[cut].reshape(8 * cols, 128)).astype(BF)
        delta[8 * cols * p : 8 * cols * (p + 1), :] = d
        send_back(p, grad, d, 1, wb, sinv, rinv, direct, usta, usrc)
    store_edges(usta, usrc, e1, e0, f1, f0)


def weight1_body(states, delta, xsum, errs, wpart):
    pairs = outer_pairs(states, delta)
    lane = iota((64, 128), 1) < 64
    wpart[0:64, :] = jnp.where(lane, pairs[0][0], pairs[1][1])
    wpart[64:128, :] = pairs[2][0]
    v = jnp.sum(errs[...] * xsum[...], axis=0, keepdims=True)
    v = jnp.broadcast_to(v, (8, 128))
    wpart[128:136, :] = v + pltpu.roll(v, 64, 1)


def gathered(direct, usta, usrc, c1, r1, c0, r0, tk, qk, hold):
    rows, cols, _ = direct.shape
    for g, part in enumerate(mix_sta(tk, usta, r0, r1)):
        hold[:, g * HW : (g + 1) * HW, :] = part.reshape(rows, HW, 128)

    def make(p):
        cut = slice(8 * p, 8 * p + 8)
        base = (direct[cut] + hold[cut]).reshape(8 * cols, 128)
        return base + mix_src(qk, usrc, c0, c1, 8 * p)

    return make


def backward0_body(direct1, usta1, usrc1, c1, r1, c0, r0, tk, qk, q, states, wb, sinv, rinv, wpart, direct, usta, usrc, e1, e0, f1, f0, pay, delta, hold):
    rows, cols, _ = q.shape
    make = gathered(direct1, usta1, usrc1, c1, r1, c0, r0, tk, qk, hold)
    for p in range(rows // 8):
        grad = make(p)
        d = (grad * q[8 * p : 8 * p + 8].reshape(8 * cols, 128)).astype(BF)
        delta[8 * cols * p : 8 * cols * (p + 1), :] = d
        send_back(p, grad, d, 0, wb, sinv, rinv, direct, usta, usrc)
    store_edges(usta, usrc, e1, e0, f1, f0)
    pairs = outer_pairs(states, delta)
    lane = iota((64, 128), 1) < 64
    pay[0:64, :] = wpart[0:64, :]
    pay[64:128, :] = jnp.where(lane, wpart[64:128, :], pairs[2][1])
    pay[128:192, :] = jnp.where(lane, pairs[0][0], pairs[1][1])
    pay[192:200, :] = wpart[128:136, :]
    pay[200:, :] = jnp.zeros((pay.shape[0] - 200, 128), F32)


def last_body(direct, usta, usrc, c1, r1, c0, r0, tk, qk, out, hold):
    make = gathered(direct, usta, usrc, c1, r1, c0, r0, tk, qk, hold)
    cols = direct.shape[1]
    for p in range(direct.shape[0] // 8):
        out[8 * p : 8 * p + 8] = make(p).astype(BF).reshape(8, cols, 128)


def sum_body(x, out):
    out[...] = jnp.broadcast_to(jnp.sum(x[...], axis=0)[None], out.shape)


def unpack_body(factor, x, w, v):
    flat = x[...].reshape(-1, 128) * factor
    first = flat[0:64]
    second = flat[64:128]
    third = flat[128:192]
    w[1, 0] = first[:, :64]
    w[1, 1] = pltpu.roll(first, 64, 1)[:, :64]
    w[1, 2] = second[:, :64]
    w[0, 2] = pltpu.roll(second, 64, 1)[:, :64]
    w[0, 0] = third[:, :64]
    w[0, 1] = pltpu.roll(third, 64, 1)[:, :64]
    v[...] = flat[192:193, :64]


def scratch_call(body, outs, scratch, *args, away=0):
    vm = pl.BlockSpec(memory_space=pltpu.VMEM)
    return pl.pallas_call(
        body,
        out_shape=[jax.ShapeDtypeStruct(s, d) for s, d in outs],
        in_specs=[pl.BlockSpec(memory_space=pl.ANY)] * away + [vm] * (len(args) - away),
        out_specs=[vm] * len(outs),
        scratch_shapes=scratch,
        compiler_params=pltpu.CompilerParams(vmem_limit_bytes=VMEM_LIMIT),
    )(*args)


def pairs_of(axis):
    count = 1
    for name in axis if isinstance(axis, tuple) else (axis,):
        count *= lax.axis_size(name)
    inner = [(i, i ^ 1) for i in range(count)]
    outer = [(i, ((i + 1) ^ 1) - 1) for i in range(1, count - 1)]
    return inner, outer


def halo(e1, e0, f1, f0):
    src0, src1 = pairs_of(SRC)
    sta0, sta1 = pairs_of("sta")
    return (
        lax.ppermute(e1, SRC, src1),
        lax.ppermute(f1, "sta", sta1),
        lax.ppermute(e0, SRC, src0),
        lax.ppermute(f0, "sta", sta0),
    )


def shards(features, station_lists, station_counts, source_lists, source_counts, picks, targets, layer_weights, readout_vector):
    rows, cols, channels = features.shape
    n_sta = lax.axis_size("sta")
    n_z = lax.axis_size("z")
    n_plane = n_sta * lax.axis_size("xh")
    whole = (rows, cols, channels)
    edge_outs = [((rows, HW, channels), BF)] * 2 + [((HW, cols, channels), BF)] * 2
    ext_sta, ext_src = rows + 2 * HW, cols + 2 * HW
    tables = (station_lists, station_counts.reshape(1, -1), source_lists, source_counts.reshape(1, -1))

    edges = scratch_call(edge_body, edge_outs, [pltpu.SemaphoreType.DMA((4,))], features, away=1)
    sk, rk, sinv, rinv, wf = call(
        lambda *refs: prep0_body(rows, cols, *refs),
        [
            ((rows * HW, ext_sta * HW), BF),
            ((4 * cols, 4 * ext_src), BF),
            ((rows * HW, channels), F32),
            ((4 * cols, channels), F32),
            ((LAYERS, 3 * channels, channels), BF),
        ],
        *tables,
        layer_weights,
    )
    state_outs = [((rows, cols, 3 * channels), BF), (whole, F32)]
    h1, *edges, states0, q0 = call(
        forward0_body, [(whole, BF)] + edge_outs + state_outs, features, *halo(*edges), sk, rk, sinv, rinv, wf
    )
    tk, qk, wb, px, cnt, tgt, rl = scratch_call(
        lambda *refs: prep1_body(rows, cols, *refs),
        [
            ((rows * HW, ext_sta * HW), BF),
            ((4 * cols, 4 * ext_src), BF),
            ((LAYERS, channels, 3 * channels), BF),
            (whole, BF),
            ((8, channels), F32),
            ((8, cols), F32),
            ((8, channels), F32),
        ],
        [],
        states0,
        *tables,
        picks,
        targets,
        layer_weights,
        readout_vector.reshape(1, -1),
        away=1,
    )
    states1, q1, xsum, block = call(
        forward1_body,
        state_outs + [((cols, channels), F32), ((n_sta, 8, channels), F32)],
        h1,
        *halo(*edges),
        sk,
        rk,
        sinv,
        rinv,
        wf,
        px,
        cnt,
        rl,
    )
    total = lax.all_to_all(block, "sta", 0, 0)
    grad_outs = [(whole, F32), (whole, BF), (whole, BF)] + edge_outs
    flat = ((rows * cols, channels), BF)
    likelihood, direct, usta, usrc, *edges, errs, delta = call(
        backward1_body,
        [((2, cols), F32)] + grad_outs + [((cols, channels), F32), flat],
        total,
        tgt,
        px,
        q1,
        rl,
        wb,
        sinv,
        rinv,
    )
    (wpart,) = call(weight1_body, [((136, channels), F32)], states1, delta, xsum, errs)
    per = -(-200 // (8 * n_plane)) * 8
    direct, usta, usrc, *edges, pay = scratch_call(
        backward0_body,
        grad_outs + [((per * n_plane, channels), F32)],
        [pltpu.VMEM(*flat), pltpu.VMEM(whole, F32)],
        direct,
        usta,
        usrc,
        *halo(*edges),
        tk,
        qk,
        q0,
        states0,
        wb,
        sinv,
        rinv,
        wpart,
    )
    (feature_grad,) = scratch_call(
        last_body, [(whole, BF)], [pltpu.VMEM(whole, F32)], direct, usta, usrc, *halo(*edges), tk, qk
    )
    part = lax.all_to_all(pay.reshape(n_plane, per, channels), PLANE, 0, 0)
    (part,) = call(sum_body, [((n_z, per, channels), F32)], part)
    part = lax.all_to_all(part, "z", 0, 0)
    (part,) = call(sum_body, [((n_plane, per, channels), F32)], part)
    part = lax.all_to_all(part, PLANE, 0, 0)
    nodes = float(rows * n_sta * cols * lax.axis_size("z") * lax.axis_size("xh"))
    feature = layer_weights.shape[-1]
    weight_grad, vector_grad = call(
        lambda *refs: unpack_body(nodes**-0.5, *refs),
        [(layer_weights.shape, F32), ((1, feature), F32)],
        part,
    )
    return likelihood, feature_grad, weight_grad, vector_grad.reshape(feature)


def solution(mesh):
    n_sta, n_src = mesh.devices.shape
    near = 2
    fine = Mesh(mesh.devices.reshape(n_sta, n_src // near, near), ("sta",) + SRC)
    in_specs = (P("sta", SRC, None), P(), P(), P(), P(), P(None, "sta"), P(None, SRC), P(), P())
    out_specs = (P(None, SRC), P("sta", SRC, None), P(), P())
    return jax.shard_map(shards, mesh=fine, in_specs=in_specs, out_specs=out_specs, check_vma=False)
```

```python
import jax
import jax.numpy as jnp
from jax import lax
from jax.experimental import pallas as pl
from jax.experimental.pallas import tpu as pltpu
from jax.sharding import Mesh
from jax.sharding import PartitionSpec as P

LAYERS = 2
HW = 16
BF = jnp.bfloat16
F32 = jnp.float32
PLANE = ("sta", "xh")
SRC = ("z", "xh")
NT = (((1,), (1,)), ((), ()))
TN = (((0,), (0,)), ((), ()))
VMEM_LIMIT = 16 * 1024 * 1024


def iota(shape, dim):
    return lax.broadcasted_iota(jnp.int32, shape, dim)


def dot(a, b):
    return jnp.dot(a, b, preferred_element_type=F32)


def dot_nt(a, b, precision=None):
    return lax.dot_general(a, b, NT, precision=precision, preferred_element_type=F32)


def onehot(mask):
    return jnp.where(mask, 1.0, 0.0).astype(BF)


def call(body, outs, *args):
    vm = pl.BlockSpec(memory_space=pltpu.VMEM)
    return pl.pallas_call(
        body,
        out_shape=[jax.ShapeDtypeStruct(s, d) for s, d in outs],
        in_specs=[vm] * len(args),
        out_specs=[vm] * len(outs),
        compiler_params=pltpu.CompilerParams(vmem_limit_bytes=VMEM_LIMIT),
    )(*args)


def even(axis):
    at = jnp.int32(0)
    for name in axis if isinstance(axis, tuple) else (axis,):
        at = at * lax.axis_size(name) + lax.axis_index(name)
    return (at & 1) == 0, at


def offsets(spot, own, flag):
    jump = own + HW
    first = jnp.where(flag, spot, spot - jump)
    second = jnp.where(flag, spot - HW - jump, spot - HW)
    return jnp.where(spot < own, spot, jnp.where(spot < own + HW, first, second))


def table_rows(lists_t, counts, first, rows, own, flag):
    width, total = lists_t.shape
    hit = onehot(iota((rows, total), 1) == offsets(iota((rows, total), 0), own, flag) + first)
    entries = lists_t[...]
    coarse = dot_nt(hit, (entries >> 5).astype(F32).astype(BF))
    fine = dot_nt(hit, (entries & 31).astype(F32).astype(BF))
    every = jnp.broadcast_to(counts[...].astype(F32), (128, total)).astype(BF)
    return (coarse * 32.0 + fine).astype(jnp.int32), dot_nt(hit, every)


def list_counts(lists, counts, first, places):
    span = places.shape[1]
    shifted = lists - first
    acc = jnp.zeros(places.shape, F32)
    for k in range(lists.shape[1]):
        hit = (shifted[:, k : k + 1] == places) & (counts[:, :span] > k)
        acc = acc + jnp.where(hit, 1.0, 0.0)
    return acc.astype(BF)


def gather_counts(lists_t, counts_ref, first, own, flag):
    lists, counts = table_rows(lists_t, counts_ref, first, own, own, flag)
    return list_counts(lists, counts, first, offsets(iota((own, own + 2 * HW), 1), own, flag)), counts


def scatter_counts(lists_t, counts_ref, first, own, flag):
    ext = own + 2 * HW
    lists, counts = table_rows(lists_t, counts_ref, first, ext, own, flag)
    return list_counts(lists, counts, first, iota((ext, own), 1))


def wide_sta(mix, target, form, own):
    ext = own + 2 * HW
    step = 128
    per = step // HW
    spread_cols = onehot(iota((ext, ext * HW), 1) >> 4 == iota((ext, ext * HW), 0))
    lane_mask = (iota((step, ext * HW), 0) & 15) == (iota((step, ext * HW), 1) & 15)
    for part in range(own * HW // step):
        pick_rows = onehot((iota((step, own), 0) >> 4) + part * per == iota((step, own), 1))
        full = dot(form(pick_rows, mix).astype(BF), spread_cols)
        target[part * step : (part + 1) * step, :] = jnp.where(lane_mask, full, 0.0).astype(BF)


def src_picks(own):
    return onehot((iota((4 * own, own), 0) & (own - 1)) == iota((4 * own, own), 1))


def wide_src(mix, target, form, own):
    ext = own + 2 * HW
    spread_cols = onehot((iota((ext, 4 * ext), 1) & (ext - 1)) == iota((ext, 4 * ext), 0))
    block_mask = (iota((4 * own, 4 * ext), 0) >> 5) == (iota((4 * own, 4 * ext), 1) >> 6)
    full = dot(form(src_picks(own), mix).astype(BF), spread_cols)
    target[...] = jnp.where(block_mask, full, 0.0).astype(BF)


def doubling(feature):
    channels = 2 * feature
    return onehot((iota((feature, channels), 1) & (feature - 1)) == iota((feature, channels), 0))


def fetch(sources, targets, sems):
    copies = [pltpu.make_async_copy(a, b, sems.at[n]) for n, (a, b) in enumerate(zip(sources, targets))]
    for copy in copies:
        copy.start()
    return copies


def prep0_body(sta_rows, src_rows, *refs):
    (sk, rk, sinv, rinv, wf, slists, scounts, rlists, rcounts, weights, sems) = refs[5:]
    copies = fetch(refs[:5], refs[10:15], sems)
    for copy in copies[:4]:
        copy.wait()
    flag, at = even("sta")
    gather, counts = gather_counts(slists, scounts, at * sta_rows, sta_rows, flag)
    wide_sta(gather, sk, dot, sta_rows)
    pick_rows = onehot((iota((sta_rows * HW, sta_rows), 0) >> 4) == iota((sta_rows * HW, sta_rows), 1))
    sinv[...] = 1.0 / dot(pick_rows, counts.astype(BF))
    flag, at = even(SRC)
    gather, counts = gather_counts(rlists, rcounts, at * src_rows, src_rows, flag)
    wide_src(gather, rk, dot, src_rows)
    rinv[...] = 1.0 / dot(src_picks(src_rows), counts.astype(BF))
    copies[4].wait()
    feature = weights.shape[-1]
    channels = 2 * feature
    twice = doubling(feature)
    left = iota((feature, channels), 1) < feature
    for layer in range(LAYERS):
        for which in range(3):
            plain = dot(weights[layer, which], twice)
            at = which * channels
            wf[layer, at : at + feature, :] = jnp.where(left, plain, 0.0).astype(BF)
            wf[layer, at + feature : at + channels, :] = jnp.where(left, 0.0, plain).astype(BF)


def prep1_body(sta_rows, src_rows, *refs):
    sources = refs[:4]
    (wb, px, cnt, tgt, rl) = refs[5:10]
    picks, targets, weights, readout = refs[10:14]
    for copy in fetch(sources, refs[10:14], refs[14]):
        copy.wait()
    feature = weights.shape[-1]
    channels = 2 * feature
    unit = onehot(iota((feature, feature), 0) == iota((feature, feature), 1))
    left = iota((feature, channels), 1) < feature
    for layer in range(LAYERS):
        for which in range(3):
            matrix = weights[layer, which]
            turned = dot_nt(unit, jnp.concatenate([matrix, matrix], 0))
            at = which * channels
            wb[layer, :feature, at : at + channels] = jnp.where(left, turned, 0.0).astype(BF)
            wb[layer, feature:, at : at + channels] = jnp.where(left, 0.0, turned).astype(BF)
    twice = doubling(feature)
    rl[...] = dot(jnp.broadcast_to(readout[...].astype(F32), (16, feature)).astype(BF), twice)[:8]

    window = iota((16, sta_rows), 0)
    picked = picks[...].astype(F32)
    rows = jnp.where(window == 0, picked[0:1, :], jnp.where(window == 1, picked[1:2, :], 0.0)).astype(BF)
    choose = onehot((iota((16, channels), 1) >> 6) == iota((16, channels), 0))
    chunk = 256
    for part in range(sta_rows * src_rows // chunk):
        at = part * chunk
        own = onehot((iota((chunk, sta_rows), 0) + at) >> 5 == iota((chunk, sta_rows), 1))
        wide = dot(dot_nt(own, rows).astype(BF), choose).astype(BF)
        span = chunk // src_rows
        px[part * span : (part + 1) * span] = wide.reshape(span, src_rows, channels)
    cnt[...] = dot(rows, jnp.ones((sta_rows, channels), BF))[:8]
    line = iota((8, src_rows), 0)
    aims = targets[...]
    tgt[...] = jnp.where(line == 0, aims[0:1, :], jnp.where(line == 1, aims[1:2, :], 0.0))


def starts(axis, own):
    flag, _ = even(axis)
    last = jnp.int32(own - HW)
    none = jnp.int32(0)
    return [pl.multiple_of(jnp.where(f, last, none), HW) for f in (flag, jnp.logical_not(flag))]


def edge_body(x, c1, c0, r1, r0, sems):
    rows, cols, _ = x.shape
    s0, s1 = starts(SRC, cols)
    t0, t1 = starts("sta", rows)
    copies = [
        pltpu.make_async_copy(x.at[:, pl.ds(s1, HW)], c1, sems.at[0]),
        pltpu.make_async_copy(x.at[:, pl.ds(s0, HW)], c0, sems.at[1]),
        pltpu.make_async_copy(x.at[pl.ds(t1, HW)], r1, sems.at[2]),
        pltpu.make_async_copy(x.at[pl.ds(t0, HW)], r0, sems.at[3]),
    ]
    for copy in copies:
        copy.start()
    for copy in copies:
        copy.wait()


def store_edges(by_row, by_col, c1, c0, r1, r0):
    s0, s1 = starts(SRC, by_col.shape[1])
    t0, t1 = starts("sta", by_row.shape[0])
    c1[...] = by_col[:, pl.ds(s1, HW)]
    c0[...] = by_col[:, pl.ds(s0, HW)]
    r1[...] = by_row[pl.ds(t1, HW)]
    r0[...] = by_row[pl.ds(t0, HW)]


def mix_sta(mix, own, r0, r1):
    span = own.shape[0] + 2 * HW
    parts = []
    for g in range(own.shape[1] // HW):
        cut = slice(g * HW, (g + 1) * HW)
        parts.append(jnp.concatenate([own[:, cut], r0[:, cut], r1[:, cut]], 0).reshape(span * HW, 128))
    out = dot(mix[...], jnp.concatenate(parts, 1))
    return [out[:, g * 128 : (g + 1) * 128] for g in range(len(parts))]


def mix_src(mix, own, c0, c1, first):
    parts = []
    for at in (first, first + 4):
        cut = slice(at, at + 4)
        joined = jnp.concatenate([own[cut], c0[cut], c1[cut]], 1)
        parts.append(joined.reshape(4 * joined.shape[1], 128))
    out = dot(mix[...], jnp.concatenate(parts, 1))
    return jnp.concatenate([out[:, :128], out[:, 128:]], 0)


def forward_parts(h, c1, r1, c0, r0, sk, rk, sinv, rinv, wf, states, keep, layer):
    rows, cols, _ = h.shape
    for g, part in enumerate(mix_sta(sk, h, r0, r1)):
        mean = (part * sinv[...]).astype(BF).reshape(rows, HW, 128)
        states[:, g * HW : (g + 1) * HW, 128:256] = mean
    states[:, :, :128] = h[...]
    both = jnp.concatenate([rinv[...], rinv[...]], 0)
    for p in range(rows // 8):
        cut = slice(8 * p, 8 * p + 8)
        mean = (mix_src(rk, h, c0, c1, 8 * p) * both).astype(BF)
        states[cut, :, 256:384] = mean.reshape(8, cols, 128)
        z = dot(states[cut].reshape(8 * cols, 384), wf[layer])
        t = jnp.tanh(z)
        keep[cut] = (1.0 - t * t).reshape(8, cols, 128)
        before = h[cut].reshape(8 * cols, 128).astype(F32)
        yield cut, (before + t).astype(BF)


def forward0_body(h, c1, r1, c0, r0, sk, rk, sinv, rinv, wf, nxt, e1, e0, f1, f0, states, keep):
    cols = h.shape[1]
    for cut, after in forward_parts(h, c1, r1, c0, r0, sk, rk, sinv, rinv, wf, states, keep, 0):
        nxt[cut] = after.reshape(8, cols, 128)
    store_edges(nxt, nxt, e1, e0, f1, f0)


def forward1_body(h, c1, r1, c0, r0, sk, rk, sinv, rinv, wf, px, cnt, rl, states, keep, xsum, block):
    cols = h.shape[1]
    acc = jnp.zeros((cols, 128), F32)
    for cut, after in forward_parts(h, c1, r1, c0, r0, sk, rk, sinv, rinv, wf, states, keep, 1):
        part = after.astype(F32).reshape(8, cols, 128) * px[cut].astype(F32)
        acc = acc + jnp.sum(part, axis=0)
    xsum[...] = acc
    read = jnp.where((iota((8, 128), 1) >> 6) == iota((8, 128), 0), rl[...], 0.0)
    padded = jnp.concatenate([acc, jnp.zeros((128 - cols, 128), F32)], 0)
    sums = dot_nt(read, padded, precision=lax.Precision.HIGHEST)
    mixed = jnp.where(iota((8, 128), 1) < 64, sums, cnt[...])
    block[...] = jnp.broadcast_to(mixed[None], block.shape)


def send_back(p, grad, d, layer, wb, sinv, rinv, direct, usta, usrc):
    cols = usta.shape[1]
    cut = slice(8 * p, 8 * p + 8)
    both = jnp.concatenate([rinv[...], rinv[...]], 0)
    u = dot(d, wb[layer])
    direct[cut] = (grad + u[:, :128]).reshape(8, cols, 128)
    scale = sinv[8 * HW * p : 8 * HW * (p + 1), :].reshape(8, HW, 128)
    scale = jnp.concatenate([scale] * (cols // HW), 1)
    usta[cut] = (u[:, 128:256].reshape(8, cols, 128) * scale).astype(BF)
    usrc[cut] = (u[:, 256:384] * both).astype(BF).reshape(8, cols, 128)


def outer_pairs(states, delta):
    rows, cols, _ = states.shape
    flat = states[...].reshape(rows * cols, 384)
    outer = lax.dot_general(flat, delta[...], TN, preferred_element_type=F32)
    pairs = []
    for which in range(3):
        top = outer[which * 128 : which * 128 + 64]
        low = outer[which * 128 + 64 : which * 128 + 128]
        pairs.append((top + pltpu.roll(low, 64, 1), pltpu.roll(top, 64, 1) + low))
    return pairs


def backward1_body(total, tgt, px, q, rl, wb, sinv, rinv, lik, direct, usta, usrc, e1, e0, f1, f0, errs, delta):
    rows, cols, _ = q.shape
    sums = jnp.sum(total[...], axis=0)
    counts = pltpu.roll(sums, 64, 1)[:, :cols]
    logits = sums[:, :cols] / jnp.sqrt(jnp.maximum(counts, 1.0))
    lik[...] = logits[:2, :]
    error = jax.nn.sigmoid(logits) - tgt[...]
    error = jnp.concatenate([error, jnp.zeros((8, cols), F32)], 0).astype(BF)
    unit = onehot(iota((cols, cols), 0) == iota((cols, cols), 1))
    choose = onehot((iota((16, 128), 1) >> 6) == iota((16, 128), 0))
    wide = dot(dot_nt(unit, error).astype(BF), choose)
    errs[...] = wide
    read = rl[0:1, :]
    for p in range(rows // 8):
        cut = slice(8 * p, 8 * p + 8)
        score = px[cut].astype(F32) * wide[None]
        grad = score.reshape(8 * cols, 128) * read
        d = (grad * q[cut].reshape(8 * cols, 128)).astype(BF)
        delta[8 * cols * p : 8 * cols * (p + 1), :] = d
        send_back(p, grad, d, 1, wb, sinv, rinv, direct, usta, usrc)
    store_edges(usta, usrc, e1, e0, f1, f0)


def weight1_body(states, delta, xsum, errs, slists, scounts, rlists, rcounts, wpart, tk, qk):
    sta_rows, src_rows, _ = states.shape
    flag, at = even("sta")
    wide_sta(scatter_counts(slists, scounts, at * sta_rows, sta_rows, flag), tk, dot_nt, sta_rows)
    flag, at = even(SRC)
    wide_src(scatter_counts(rlists, rcounts, at * src_rows, src_rows, flag), qk, dot_nt, src_rows)
    pairs = outer_pairs(states, delta)
    lane = iota((64, 128), 1) < 64
    wpart[0:64, :] = jnp.where(lane, pairs[0][0], pairs[1][1])
    wpart[64:128, :] = pairs[2][0]
    v = jnp.sum(errs[...] * xsum[...], axis=0, keepdims=True)
    v = jnp.broadcast_to(v, (8, 128))
    wpart[128:136, :] = v + pltpu.roll(v, 64, 1)


def gathered(direct, usta, usrc, c1, r1, c0, r0, tk, qk, hold):
    rows, cols, _ = direct.shape
    for g, part in enumerate(mix_sta(tk, usta, r0, r1)):
        hold[:, g * HW : (g + 1) * HW, :] = part.reshape(rows, HW, 128)

    def make(p):
        cut = slice(8 * p, 8 * p + 8)
        base = (direct[cut] + hold[cut]).reshape(8 * cols, 128)
        return base + mix_src(qk, usrc, c0, c1, 8 * p)

    return make


def backward0_body(direct1, usta1, usrc1, c1, r1, c0, r0, tk, qk, q, states, wb, sinv, rinv, wpart, direct, usta, usrc, e1, e0, f1, f0, pay, delta, hold):
    rows, cols, _ = q.shape
    make = gathered(direct1, usta1, usrc1, c1, r1, c0, r0, tk, qk, hold)
    for p in range(rows // 8):
        grad = make(p)
        d = (grad * q[8 * p : 8 * p + 8].reshape(8 * cols, 128)).astype(BF)
        delta[8 * cols * p : 8 * cols * (p + 1), :] = d
        send_back(p, grad, d, 0, wb, sinv, rinv, direct, usta, usrc)
    store_edges(usta, usrc, e1, e0, f1, f0)
    pairs = outer_pairs(states, delta)
    lane = iota((64, 128), 1) < 64
    pay[0:64, :] = wpart[0:64, :]
    pay[64:128, :] = jnp.where(lane, wpart[64:128, :], pairs[2][1])
    pay[128:192, :] = jnp.where(lane, pairs[0][0], pairs[1][1])
    pay[192:200, :] = wpart[128:136, :]
    pay[200:, :] = jnp.zeros((pay.shape[0] - 200, 128), F32)


def last_body(direct, usta, usrc, c1, r1, c0, r0, tk, qk, out, hold):
    make = gathered(direct, usta, usrc, c1, r1, c0, r0, tk, qk, hold)
    cols = direct.shape[1]
    for p in range(direct.shape[0] // 8):
        out[8 * p : 8 * p + 8] = make(p).astype(BF).reshape(8, cols, 128)


def sum_body(x, out):
    out[...] = jnp.broadcast_to(jnp.sum(x[...], axis=0)[None], out.shape)


def unpack_body(factor, x, w, v):
    flat = x[...].reshape(-1, 128) * factor
    first = flat[0:64]
    second = flat[64:128]
    third = flat[128:192]
    w[1, 0] = first[:, :64]
    w[1, 1] = pltpu.roll(first, 64, 1)[:, :64]
    w[1, 2] = second[:, :64]
    w[0, 2] = pltpu.roll(second, 64, 1)[:, :64]
    w[0, 0] = third[:, :64]
    w[0, 1] = pltpu.roll(third, 64, 1)[:, :64]
    v[...] = flat[192:193, :64]


def scratch_call(body, outs, scratch, *args, away=0):
    vm = pl.BlockSpec(memory_space=pltpu.VMEM)
    args = [pltpu.with_memory_space_constraint(x, pltpu.HBM) if n < away else x for n, x in enumerate(args)]
    return pl.pallas_call(
        body,
        out_shape=[jax.ShapeDtypeStruct(s, d) for s, d in outs],
        in_specs=[pl.BlockSpec(memory_space=pltpu.HBM)] * away + [vm] * (len(args) - away),
        out_specs=[vm] * len(outs),
        scratch_shapes=scratch,
        compiler_params=pltpu.CompilerParams(vmem_limit_bytes=VMEM_LIMIT),
    )(*args)


def pairs_of(axis):
    count = 1
    for name in axis if isinstance(axis, tuple) else (axis,):
        count *= lax.axis_size(name)
    inner = [(i, i ^ 1) for i in range(count)]
    outer = [(i, ((i + 1) ^ 1) - 1) for i in range(1, count - 1)]
    return inner, outer


def halo(e1, e0, f1, f0):
    src0, src1 = pairs_of(SRC)
    sta0, sta1 = pairs_of("sta")
    return (
        lax.ppermute(e1, SRC, src1),
        lax.ppermute(f1, "sta", sta1),
        lax.ppermute(e0, SRC, src0),
        lax.ppermute(f0, "sta", sta0),
    )


def shards(features, station_lists, station_counts, source_lists, source_counts, picks, targets, layer_weights, readout_vector):
    rows, cols, channels = features.shape
    n_sta = lax.axis_size("sta")
    n_z = lax.axis_size("z")
    n_plane = n_sta * lax.axis_size("xh")
    whole = (rows, cols, channels)
    edge_outs = [((rows, HW, channels), BF)] * 2 + [((HW, cols, channels), BF)] * 2
    ext_sta, ext_src = rows + 2 * HW, cols + 2 * HW
    tables = (station_lists.T, station_counts.reshape(1, -1), source_lists.T, source_counts.reshape(1, -1))

    edges = scratch_call(edge_body, edge_outs, [pltpu.SemaphoreType.DMA((4,))], features, away=1)
    sk, rk, sinv, rinv, wf = scratch_call(
        lambda *refs: prep0_body(rows, cols, *refs),
        [
            ((rows * HW, ext_sta * HW), BF),
            ((4 * cols, 4 * ext_src), BF),
            ((rows * HW, channels), F32),
            ((4 * cols, channels), F32),
            ((LAYERS, 3 * channels, channels), BF),
        ],
        [pltpu.VMEM(x.shape, x.dtype) for x in (*tables, layer_weights)] + [pltpu.SemaphoreType.DMA((5,))],
        *tables,
        layer_weights,
        away=5,
    )
    state_outs = [((rows, cols, 3 * channels), BF), (whole, F32)]
    h1, *edges, states0, q0 = call(
        forward0_body, [(whole, BF)] + edge_outs + state_outs, features, *halo(*edges), sk, rk, sinv, rinv, wf
    )
    small = (picks, targets, layer_weights, readout_vector.reshape(1, -1))
    wb, px, cnt, tgt, rl = scratch_call(
        lambda *refs: prep1_body(rows, cols, *refs),
        [
            ((LAYERS, channels, 3 * channels), BF),
            (whole, BF),
            ((8, channels), F32),
            ((8, cols), F32),
            ((8, channels), F32),
        ],
        [pltpu.VMEM(x.shape, x.dtype) for x in small] + [pltpu.SemaphoreType.DMA((4,))],
        *small,
        states0,
        away=4,
    )
    states1, q1, xsum, block = call(
        forward1_body,
        state_outs + [((cols, channels), F32), ((n_sta, 8, channels), F32)],
        h1,
        *halo(*edges),
        sk,
        rk,
        sinv,
        rinv,
        wf,
        px,
        cnt,
        rl,
    )
    total = lax.all_to_all(block, "sta", 0, 0)
    grad_outs = [(whole, F32), (whole, BF), (whole, BF)] + edge_outs
    flat = ((rows * cols, channels), BF)
    likelihood, direct, usta, usrc, *edges, errs, delta = call(
        backward1_body,
        [((2, cols), F32)] + grad_outs + [((cols, channels), F32), flat],
        total,
        tgt,
        px,
        q1,
        rl,
        wb,
        sinv,
        rinv,
    )
    wpart, tk, qk = call(
        weight1_body,
        [((136, channels), F32), ((rows * HW, ext_sta * HW), BF), ((4 * cols, 4 * ext_src), BF)],
        states1,
        delta,
        xsum,
        errs,
        *tables,
    )
    per = -(-200 // (8 * n_plane)) * 8
    direct, usta, usrc, *edges, pay = scratch_call(
        backward0_body,
        grad_outs + [((per * n_plane, channels), F32)],
        [pltpu.VMEM(*flat), pltpu.VMEM(whole, F32)],
        direct,
        usta,
        usrc,
        *halo(*edges),
        tk,
        qk,
        q0,
        states0,
        wb,
        sinv,
        rinv,
        wpart,
    )
    (feature_grad,) = scratch_call(
        last_body, [(whole, BF)], [pltpu.VMEM(whole, F32)], direct, usta, usrc, *halo(*edges), tk, qk
    )
    part = lax.all_to_all(pay.reshape(n_plane, per, channels), PLANE, 0, 0)
    (part,) = call(sum_body, [((n_z, per, channels), F32)], part)
    part = lax.all_to_all(part, "z", 0, 0)
    (part,) = call(sum_body, [((n_plane, per, channels), F32)], part)
    part = lax.all_to_all(part, PLANE, 0, 0)
    nodes = float(rows * n_sta * cols * lax.axis_size("z") * lax.axis_size("xh"))
    feature = layer_weights.shape[-1]
    weight_grad, vector_grad = call(
        lambda *refs: unpack_body(nodes**-0.5, *refs),
        [(layer_weights.shape, F32), ((1, feature), F32)],
        part,
    )
    return likelihood, feature_grad, weight_grad, vector_grad.reshape(feature)


def solution(mesh):
    n_sta, n_src = mesh.devices.shape
    near = 2
    fine = Mesh(mesh.devices.reshape(n_sta, n_src // near, near), ("sta",) + SRC)
    in_specs = (P("sta", SRC, None), P(), P(), P(), P(), P(None, "sta"), P(None, SRC), P(), P())
    out_specs = (P(None, SRC), P("sta", SRC, None), P(), P())
    return jax.shard_map(shards, mesh=fine, in_specs=in_specs, out_specs=out_specs, check_vma=False)
```

```python
import jax
import jax.numpy as jnp
from jax import lax
from jax.experimental import pallas as pl
from jax.experimental.pallas import tpu as pltpu
from jax.sharding import Mesh
from jax.sharding import PartitionSpec as P

LAYERS = 2
HW = 16
BF = jnp.bfloat16
F32 = jnp.float32
PLANE = ("sta", "xh")
SRC = ("z", "xh")
NT = (((1,), (1,)), ((), ()))
TN = (((0,), (0,)), ((), ()))
VMEM_LIMIT = 16 * 1024 * 1024


def iota(shape, dim):
    return lax.broadcasted_iota(jnp.int32, shape, dim)


def dot(a, b):
    return jnp.dot(a, b, preferred_element_type=F32)


def dot_nt(a, b, precision=None):
    return lax.dot_general(a, b, NT, precision=precision, preferred_element_type=F32)


def onehot(mask):
    return jnp.where(mask, 1.0, 0.0).astype(BF)


def call(body, outs, *args):
    vm = pl.BlockSpec(memory_space=pltpu.VMEM)
    return pl.pallas_call(
        body,
        out_shape=[jax.ShapeDtypeStruct(s, d) for s, d in outs],
        in_specs=[vm] * len(args),
        out_specs=[vm] * len(outs),
        compiler_params=pltpu.CompilerParams(vmem_limit_bytes=VMEM_LIMIT),
    )(*args)


def even(axis):
    at = jnp.int32(0)
    for name in axis if isinstance(axis, tuple) else (axis,):
        at = at * lax.axis_size(name) + lax.axis_index(name)
    return (at & 1) == 0, at


def offsets(spot, own, flag):
    jump = own + HW
    first = jnp.where(flag, spot, spot - jump)
    second = jnp.where(flag, spot - HW - jump, spot - HW)
    return jnp.where(spot < own, spot, jnp.where(spot < own + HW, first, second))


def table_rows(lists_t, counts, first, rows, own, flag):
    width, total = lists_t.shape
    hit = onehot(iota((rows, total), 1) == offsets(iota((rows, total), 0), own, flag) + first)
    entries = lists_t[...]
    coarse = dot_nt(hit, (entries >> 5).astype(F32).astype(BF))
    fine = dot_nt(hit, (entries & 31).astype(F32).astype(BF))
    every = jnp.broadcast_to(counts[...].astype(F32), (128, total)).astype(BF)
    return (coarse * 32.0 + fine).astype(jnp.int32), dot_nt(hit, every)


def list_counts(lists, counts, first, places):
    span = places.shape[1]
    shifted = lists - first
    acc = jnp.zeros(places.shape, F32)
    for k in range(lists.shape[1]):
        hit = (shifted[:, k : k + 1] == places) & (counts[:, :span] > k)
        acc = acc + jnp.where(hit, 1.0, 0.0)
    return acc.astype(BF)


def gather_counts(lists_t, counts_ref, first, own, flag):
    lists, counts = table_rows(lists_t, counts_ref, first, own, own, flag)
    return list_counts(lists, counts, first, offsets(iota((own, own + 2 * HW), 1), own, flag)), counts


def scatter_counts(lists_t, counts_ref, first, own, flag):
    ext = own + 2 * HW
    lists, counts = table_rows(lists_t, counts_ref, first, ext, own, flag)
    return list_counts(lists, counts, first, iota((ext, own), 1))


def wide_sta(mix, target, form, own):
    ext = own + 2 * HW
    step = 128
    per = step // HW
    spread_cols = onehot(iota((ext, ext * HW), 1) >> 4 == iota((ext, ext * HW), 0))
    lane_mask = (iota((step, ext * HW), 0) & 15) == (iota((step, ext * HW), 1) & 15)
    for part in range(own * HW // step):
        pick_rows = onehot((iota((step, own), 0) >> 4) + part * per == iota((step, own), 1))
        full = dot(form(pick_rows, mix).astype(BF), spread_cols)
        target[part * step : (part + 1) * step, :] = jnp.where(lane_mask, full, 0.0).astype(BF)


def src_picks(own):
    return onehot((iota((4 * own, own), 0) & (own - 1)) == iota((4 * own, own), 1))


def wide_src(mix, target, form, own):
    ext = own + 2 * HW
    spread_cols = onehot((iota((ext, 4 * ext), 1) & (ext - 1)) == iota((ext, 4 * ext), 0))
    block_mask = (iota((4 * own, 4 * ext), 0) >> 5) == (iota((4 * own, 4 * ext), 1) >> 6)
    full = dot(form(src_picks(own), mix).astype(BF), spread_cols)
    target[...] = jnp.where(block_mask, full, 0.0).astype(BF)


def doubling(feature):
    channels = 2 * feature
    return onehot((iota((feature, channels), 1) & (feature - 1)) == iota((feature, channels), 0))


def prep0_body(sta_rows, src_rows, slists, scounts, rlists, rcounts, weights, sk, rk, sinv, rinv, wf):
    flag, at = even("sta")
    gather, counts = gather_counts(slists, scounts, at * sta_rows, sta_rows, flag)
    wide_sta(gather, sk, dot, sta_rows)
    pick_rows = onehot((iota((sta_rows * HW, sta_rows), 0) >> 4) == iota((sta_rows * HW, sta_rows), 1))
    sinv[...] = 1.0 / dot(pick_rows, counts.astype(BF))
    flag, at = even(SRC)
    gather, counts = gather_counts(rlists, rcounts, at * src_rows, src_rows, flag)
    wide_src(gather, rk, dot, src_rows)
    rinv[...] = 1.0 / dot(src_picks(src_rows), counts.astype(BF))
    feature = weights.shape[-1]
    channels = 2 * feature
    twice = doubling(feature)
    left = iota((feature, channels), 1) < feature
    for layer in range(LAYERS):
        for which in range(3):
            plain = dot(weights[layer, which], twice)
            at = which * channels
            wf[layer, at : at + feature, :] = jnp.where(left, plain, 0.0).astype(BF)
            wf[layer, at + feature : at + channels, :] = jnp.where(left, 0.0, plain).astype(BF)


def prep1_body(sta_rows, src_rows, _, picks, targets, weights, readout, wb, px, cnt, tgt, rl):
    feature = weights.shape[-1]
    channels = 2 * feature
    unit = onehot(iota((feature, feature), 0) == iota((feature, feature), 1))
    left = iota((feature, channels), 1) < feature
    for layer in range(LAYERS):
        for which in range(3):
            matrix = weights[layer, which]
            turned = dot_nt(unit, jnp.concatenate([matrix, matrix], 0))
            at = which * channels
            wb[layer, :feature, at : at + channels] = jnp.where(left, turned, 0.0).astype(BF)
            wb[layer, feature:, at : at + channels] = jnp.where(left, 0.0, turned).astype(BF)
    twice = doubling(feature)
    rl[...] = dot(jnp.broadcast_to(readout[...].astype(F32), (16, feature)).astype(BF), twice)[:8]

    window = iota((16, sta_rows), 0)
    picked = picks[...].astype(F32)
    rows = jnp.where(window == 0, picked[0:1, :], jnp.where(window == 1, picked[1:2, :], 0.0)).astype(BF)
    choose = onehot((iota((16, channels), 1) >> 6) == iota((16, channels), 0))
    chunk = 256
    for part in range(sta_rows * src_rows // chunk):
        at = part * chunk
        own = onehot((iota((chunk, sta_rows), 0) + at) >> 5 == iota((chunk, sta_rows), 1))
        wide = dot(dot_nt(own, rows).astype(BF), choose).astype(BF)
        span = chunk // src_rows
        px[part * span : (part + 1) * span] = wide.reshape(span, src_rows, channels)
    cnt[...] = dot(rows, jnp.ones((sta_rows, channels), BF))[:8]
    line = iota((8, src_rows), 0)
    aims = targets[...]
    tgt[...] = jnp.where(line == 0, aims[0:1, :], jnp.where(line == 1, aims[1:2, :], 0.0))


def starts(axis, own):
    flag, _ = even(axis)
    last = jnp.int32(own - HW)
    none = jnp.int32(0)
    return [pl.multiple_of(jnp.where(f, last, none), HW) for f in (flag, jnp.logical_not(flag))]


def edge_body(count, *refs):
    x, rest = refs[0], refs[1:count]
    c1, c0, r1, r0 = refs[count : count + 4]
    sems = refs[-1]
    rows, cols, _ = x.shape
    s0, s1 = starts(SRC, cols)
    t0, t1 = starts("sta", rows)
    moves = [(x.at[:, pl.ds(s1, HW)], c1), (x.at[pl.ds(t1, HW)], r1)]
    moves += [(x.at[:, pl.ds(s0, HW)], c0), (x.at[pl.ds(t0, HW)], r0)]
    moves += list(zip(rest, refs[count + 4 : -1]))
    copies = [pltpu.make_async_copy(a, b, sems.at[n]) for n, (a, b) in enumerate(moves)]
    for copy in copies:
        copy.start()
    for copy in copies:
        copy.wait()


def store_edges(by_row, by_col, c1, c0, r1, r0):
    s0, s1 = starts(SRC, by_col.shape[1])
    t0, t1 = starts("sta", by_row.shape[0])
    c1[...] = by_col[:, pl.ds(s1, HW)]
    c0[...] = by_col[:, pl.ds(s0, HW)]
    r1[...] = by_row[pl.ds(t1, HW)]
    r0[...] = by_row[pl.ds(t0, HW)]


def mix_sta(mix, own, r0, r1):
    span = own.shape[0] + 2 * HW
    parts = []
    for g in range(own.shape[1] // HW):
        cut = slice(g * HW, (g + 1) * HW)
        parts.append(jnp.concatenate([own[:, cut], r0[:, cut], r1[:, cut]], 0).reshape(span * HW, 128))
    out = dot(mix[...], jnp.concatenate(parts, 1))
    return [out[:, g * 128 : (g + 1) * 128] for g in range(len(parts))]


def mix_src(mix, own, c0, c1, first):
    parts = []
    for at in (first, first + 4):
        cut = slice(at, at + 4)
        joined = jnp.concatenate([own[cut], c0[cut], c1[cut]], 1)
        parts.append(joined.reshape(4 * joined.shape[1], 128))
    out = dot(mix[...], jnp.concatenate(parts, 1))
    return jnp.concatenate([out[:, :128], out[:, 128:]], 0)


def forward_parts(h, c1, r1, c0, r0, sk, rk, sinv, rinv, wf, states, keep, layer):
    rows, cols, _ = h.shape
    for g, part in enumerate(mix_sta(sk, h, r0, r1)):
        mean = (part * sinv[...]).astype(BF).reshape(rows, HW, 128)
        states[:, g * HW : (g + 1) * HW, 128:256] = mean
    states[:, :, :128] = h[...]
    both = jnp.concatenate([rinv[...], rinv[...]], 0)
    for p in range(rows // 8):
        cut = slice(8 * p, 8 * p + 8)
        mean = (mix_src(rk, h, c0, c1, 8 * p) * both).astype(BF)
        states[cut, :, 256:384] = mean.reshape(8, cols, 128)
        z = dot(states[cut].reshape(8 * cols, 384), wf[layer])
        t = jnp.tanh(z)
        keep[cut] = (1.0 - t * t).reshape(8, cols, 128)
        before = h[cut].reshape(8 * cols, 128).astype(F32)
        yield cut, (before + t).astype(BF)


def forward0_body(h, c1, r1, c0, r0, sk, rk, sinv, rinv, wf, nxt, e1, e0, f1, f0, states, keep):
    cols = h.shape[1]
    for cut, after in forward_parts(h, c1, r1, c0, r0, sk, rk, sinv, rinv, wf, states, keep, 0):
        nxt[cut] = after.reshape(8, cols, 128)
    store_edges(nxt, nxt, e1, e0, f1, f0)


def forward1_body(h, c1, r1, c0, r0, sk, rk, sinv, rinv, wf, px, cnt, rl, states, keep, xsum, block):
    cols = h.shape[1]
    acc = jnp.zeros((cols, 128), F32)
    for cut, after in forward_parts(h, c1, r1, c0, r0, sk, rk, sinv, rinv, wf, states, keep, 1):
        part = after.astype(F32).reshape(8, cols, 128) * px[cut].astype(F32)
        acc = acc + jnp.sum(part, axis=0)
    xsum[...] = acc
    read = jnp.where((iota((8, 128), 1) >> 6) == iota((8, 128), 0), rl[...], 0.0)
    padded = jnp.concatenate([acc, jnp.zeros((128 - cols, 128), F32)], 0)
    sums = dot_nt(read, padded, precision=lax.Precision.HIGHEST)
    mixed = jnp.where(iota((8, 128), 1) < 64, sums, cnt[...])
    block[...] = jnp.broadcast_to(mixed[None], block.shape)


def send_back(p, grad, d, layer, wb, sinv, rinv, direct, usta, usrc):
    cols = usta.shape[1]
    cut = slice(8 * p, 8 * p + 8)
    both = jnp.concatenate([rinv[...], rinv[...]], 0)
    u = dot(d, wb[layer])
    direct[cut] = (grad + u[:, :128]).reshape(8, cols, 128)
    scale = sinv[8 * HW * p : 8 * HW * (p + 1), :].reshape(8, HW, 128)
    scale = jnp.concatenate([scale] * (cols // HW), 1)
    usta[cut] = (u[:, 128:256].reshape(8, cols, 128) * scale).astype(BF)
    usrc[cut] = (u[:, 256:384] * both).astype(BF).reshape(8, cols, 128)


def outer_pairs(states, delta):
    rows, cols, _ = states.shape
    flat = states[...].reshape(rows * cols, 384)
    outer = lax.dot_general(flat, delta[...], TN, preferred_element_type=F32)
    pairs = []
    for which in range(3):
        top = outer[which * 128 : which * 128 + 64]
        low = outer[which * 128 + 64 : which * 128 + 128]
        pairs.append((top + pltpu.roll(low, 64, 1), pltpu.roll(top, 64, 1) + low))
    return pairs


def backward1_body(total, tgt, px, q, rl, wb, sinv, rinv, lik, direct, usta, usrc, e1, e0, f1, f0, errs, delta):
    rows, cols, _ = q.shape
    sums = jnp.sum(total[...], axis=0)
    counts = pltpu.roll(sums, 64, 1)[:, :cols]
    logits = sums[:, :cols] / jnp.sqrt(jnp.maximum(counts, 1.0))
    lik[...] = logits[:2, :]
    error = jax.nn.sigmoid(logits) - tgt[...]
    error = jnp.concatenate([error, jnp.zeros((8, cols), F32)], 0).astype(BF)
    unit = onehot(iota((cols, cols), 0) == iota((cols, cols), 1))
    choose = onehot((iota((16, 128), 1) >> 6) == iota((16, 128), 0))
    wide = dot(dot_nt(unit, error).astype(BF), choose)
    errs[...] = wide
    read = rl[0:1, :]
    for p in range(rows // 8):
        cut = slice(8 * p, 8 * p + 8)
        score = px[cut].astype(F32) * wide[None]
        grad = score.reshape(8 * cols, 128) * read
        d = (grad * q[cut].reshape(8 * cols, 128)).astype(BF)
        delta[8 * cols * p : 8 * cols * (p + 1), :] = d
        send_back(p, grad, d, 1, wb, sinv, rinv, direct, usta, usrc)
    store_edges(usta, usrc, e1, e0, f1, f0)


def weight1_body(states, delta, xsum, errs, slists, scounts, rlists, rcounts, wpart, tk, qk):
    sta_rows, src_rows, _ = states.shape
    flag, at = even("sta")
    wide_sta(scatter_counts(slists, scounts, at * sta_rows, sta_rows, flag), tk, dot_nt, sta_rows)
    flag, at = even(SRC)
    wide_src(scatter_counts(rlists, rcounts, at * src_rows, src_rows, flag), qk, dot_nt, src_rows)
    pairs = outer_pairs(states, delta)
    lane = iota((64, 128), 1) < 64
    wpart[0:64, :] = jnp.where(lane, pairs[0][0], pairs[1][1])
    wpart[64:128, :] = pairs[2][0]
    v = jnp.sum(errs[...] * xsum[...], axis=0, keepdims=True)
    v = jnp.broadcast_to(v, (8, 128))
    wpart[128:136, :] = v + pltpu.roll(v, 64, 1)


def gathered(direct, usta, usrc, c1, r1, c0, r0, tk, qk, hold):
    rows, cols, _ = direct.shape
    for g, part in enumerate(mix_sta(tk, usta, r0, r1)):
        hold[:, g * HW : (g + 1) * HW, :] = part.reshape(rows, HW, 128)

    def make(p):
        cut = slice(8 * p, 8 * p + 8)
        base = (direct[cut] + hold[cut]).reshape(8 * cols, 128)
        return base + mix_src(qk, usrc, c0, c1, 8 * p)

    return make


def backward0_body(direct1, usta1, usrc1, c1, r1, c0, r0, tk, qk, q, states, wb, sinv, rinv, wpart, direct, usta, usrc, e1, e0, f1, f0, pay, delta, hold):
    rows, cols, _ = q.shape
    make = gathered(direct1, usta1, usrc1, c1, r1, c0, r0, tk, qk, hold)
    for p in range(rows // 8):
        grad = make(p)
        d = (grad * q[8 * p : 8 * p + 8].reshape(8 * cols, 128)).astype(BF)
        delta[8 * cols * p : 8 * cols * (p + 1), :] = d
        send_back(p, grad, d, 0, wb, sinv, rinv, direct, usta, usrc)
    store_edges(usta, usrc, e1, e0, f1, f0)
    pairs = outer_pairs(states, delta)
    lane = iota((64, 128), 1) < 64
    pay[0:64, :] = wpart[0:64, :]
    pay[64:128, :] = jnp.where(lane, wpart[64:128, :], pairs[2][1])
    pay[128:192, :] = jnp.where(lane, pairs[0][0], pairs[1][1])
    pay[192:200, :] = wpart[128:136, :]
    pay[200:, :] = jnp.zeros((pay.shape[0] - 200, 128), F32)


def last_body(direct, usta, usrc, c1, r1, c0, r0, tk, qk, out, hold):
    make = gathered(direct, usta, usrc, c1, r1, c0, r0, tk, qk, hold)
    cols = direct.shape[1]
    for p in range(direct.shape[0] // 8):
        out[8 * p : 8 * p + 8] = make(p).astype(BF).reshape(8, cols, 128)


def sum_body(x, out):
    out[...] = jnp.broadcast_to(jnp.sum(x[...], axis=0)[None], out.shape)


def unpack_body(factor, x, w, v):
    flat = x[...].reshape(-1, 128) * factor
    first = flat[0:64]
    second = flat[64:128]
    third = flat[128:192]
    w[1, 0] = first[:, :64]
    w[1, 1] = pltpu.roll(first, 64, 1)[:, :64]
    w[1, 2] = second[:, :64]
    w[0, 2] = pltpu.roll(second, 64, 1)[:, :64]
    w[0, 0] = third[:, :64]
    w[0, 1] = pltpu.roll(third, 64, 1)[:, :64]
    v[...] = flat[192:193, :64]


def scratch_call(body, outs, scratch, *args, away=0):
    vm = pl.BlockSpec(memory_space=pltpu.VMEM)
    args = [pltpu.with_memory_space_constraint(x, pltpu.HBM) if n < away else x for n, x in enumerate(args)]
    return pl.pallas_call(
        body,
        out_shape=[jax.ShapeDtypeStruct(s, d) for s, d in outs],
        in_specs=[pl.BlockSpec(memory_space=pltpu.HBM)] * away + [vm] * (len(args) - away),
        out_specs=[vm] * len(outs),
        scratch_shapes=scratch,
        compiler_params=pltpu.CompilerParams(vmem_limit_bytes=VMEM_LIMIT),
    )(*args)


def pairs_of(axis):
    count = 1
    for name in axis if isinstance(axis, tuple) else (axis,):
        count *= lax.axis_size(name)
    inner = [(i, i ^ 1) for i in range(count)]
    outer = [(i, ((i + 1) ^ 1) - 1) for i in range(1, count - 1)]
    return inner, outer


def halo(e1, e0, f1, f0):
    src0, src1 = pairs_of(SRC)
    sta0, sta1 = pairs_of("sta")
    return (
        lax.ppermute(e1, SRC, src1),
        lax.ppermute(f1, "sta", sta1),
        lax.ppermute(e0, SRC, src0),
        lax.ppermute(f0, "sta", sta0),
    )


def shards(features, station_lists, station_counts, source_lists, source_counts, picks, targets, layer_weights, readout_vector):
    rows, cols, channels = features.shape
    n_sta = lax.axis_size("sta")
    n_z = lax.axis_size("z")
    n_plane = n_sta * lax.axis_size("xh")
    whole = (rows, cols, channels)
    edge_outs = [((rows, HW, channels), BF)] * 2 + [((HW, cols, channels), BF)] * 2
    ext_sta, ext_src = rows + 2 * HW, cols + 2 * HW
    tables = (station_lists.T, station_counts.reshape(1, -1), source_lists.T, source_counts.reshape(1, -1))

    small = tables + (layer_weights, picks, targets, readout_vector.reshape(1, -1))
    c1, c0, r1, r0, *small = scratch_call(
        lambda *refs: edge_body(1 + len(small), *refs),
        edge_outs + [(x.shape, x.dtype) for x in small],
        [pltpu.SemaphoreType.DMA((4 + len(small),))],
        features,
        *small,
        away=1 + len(small),
    )
    edges = (c1, c0, r1, r0)
    tables, (weights, picks, targets, readout) = small[:4], small[4:]
    sk, rk, sinv, rinv, wf = scratch_call(
        lambda *refs: prep0_body(rows, cols, *refs),
        [
            ((rows * HW, ext_sta * HW), BF),
            ((4 * cols, 4 * ext_src), BF),
            ((rows * HW, channels), F32),
            ((4 * cols, channels), F32),
            ((LAYERS, 3 * channels, channels), BF),
        ],
        [],
        *tables,
        weights,
    )
    state_outs = [((rows, cols, 3 * channels), BF), (whole, F32)]
    h1, *edges, states0, q0 = call(
        forward0_body, [(whole, BF)] + edge_outs + state_outs, features, *halo(*edges), sk, rk, sinv, rinv, wf
    )
    wb, px, cnt, tgt, rl = scratch_call(
        lambda *refs: prep1_body(rows, cols, *refs),
        [
            ((LAYERS, channels, 3 * channels), BF),
            (whole, BF),
            ((8, channels), F32),
            ((8, cols), F32),
            ((8, channels), F32),
        ],
        [],
        states0,
        picks,
        targets,
        weights,
        readout,
    )
    states1, q1, xsum, block = call(
        forward1_body,
        state_outs + [((cols, channels), F32), ((n_sta, 8, channels), F32)],
        h1,
        *halo(*edges),
        sk,
        rk,
        sinv,
        rinv,
        wf,
        px,
        cnt,
        rl,
    )
    total = lax.all_to_all(block, "sta", 0, 0)
    grad_outs = [(whole, F32), (whole, BF), (whole, BF)] + edge_outs
    flat = ((rows * cols, channels), BF)
    likelihood, direct, usta, usrc, *edges, errs, delta = call(
        backward1_body,
        [((2, cols), F32)] + grad_outs + [((cols, channels), F32), flat],
        total,
        tgt,
        px,
        q1,
        rl,
        wb,
        sinv,
        rinv,
    )
    wpart, tk, qk = call(
        weight1_body,
        [((136, channels), F32), ((rows * HW, ext_sta * HW), BF), ((4 * cols, 4 * ext_src), BF)],
        states1,
        delta,
        xsum,
        errs,
        *tables,
    )
    per = -(-200 // (8 * n_plane)) * 8
    direct, usta, usrc, *edges, pay = scratch_call(
        backward0_body,
        grad_outs + [((per * n_plane, channels), F32)],
        [pltpu.VMEM(*flat), pltpu.VMEM(whole, F32)],
        direct,
        usta,
        usrc,
        *halo(*edges),
        tk,
        qk,
        q0,
        states0,
        wb,
        sinv,
        rinv,
        wpart,
    )
    (feature_grad,) = scratch_call(
        last_body, [(whole, BF)], [pltpu.VMEM(whole, F32)], direct, usta, usrc, *halo(*edges), tk, qk
    )
    part = lax.all_to_all(pay.reshape(n_plane, per, channels), PLANE, 0, 0)
    (part,) = call(sum_body, [((n_z, per, channels), F32)], part)
    part = lax.all_to_all(part, "z", 0, 0)
    (part,) = call(sum_body, [((n_plane, per, channels), F32)], part)
    part = lax.all_to_all(part, PLANE, 0, 0)
    nodes = float(rows * n_sta * cols * lax.axis_size("z") * lax.axis_size("xh"))
    feature = layer_weights.shape[-1]
    weight_grad, vector_grad = call(
        lambda *refs: unpack_body(nodes**-0.5, *refs),
        [(layer_weights.shape, F32), ((1, feature), F32)],
        part,
    )
    return likelihood, feature_grad, weight_grad, vector_grad.reshape(feature)


def solution(mesh):
    n_sta, n_src = mesh.devices.shape
    near = 2
    fine = Mesh(mesh.devices.reshape(n_sta, n_src // near, near), ("sta",) + SRC)
    in_specs = (P("sta", SRC, None), P(), P(), P(), P(), P(None, "sta"), P(None, SRC), P(), P())
    out_specs = (P(None, SRC), P("sta", SRC, None), P(), P())
    return jax.shard_map(shards, mesh=fine, in_specs=in_specs, out_specs=out_specs, check_vma=False)
```

```python
import jax
import jax.numpy as jnp
from jax import lax
from jax.experimental import pallas as pl
from jax.experimental.pallas import tpu as pltpu
from jax.sharding import Mesh
from jax.sharding import PartitionSpec as P

LAYERS = 2
HW = 16
BF = jnp.bfloat16
F32 = jnp.float32
PLANE = ("sta", "xh")
SRC = ("z", "xh")
NT = (((1,), (1,)), ((), ()))
TN = (((0,), (0,)), ((), ()))
VMEM_LIMIT = 16 * 1024 * 1024


def iota(shape, dim):
    return lax.broadcasted_iota(jnp.int32, shape, dim)


def dot(a, b):
    return jnp.dot(a, b, preferred_element_type=F32)


def dot_nt(a, b, precision=None):
    return lax.dot_general(a, b, NT, precision=precision, preferred_element_type=F32)


def onehot(mask):
    return jnp.where(mask, 1.0, 0.0).astype(BF)


def call(body, outs, *args):
    vm = pl.BlockSpec(memory_space=pltpu.VMEM)
    return pl.pallas_call(
        body,
        out_shape=[jax.ShapeDtypeStruct(s, d) for s, d in outs],
        in_specs=[vm] * len(args),
        out_specs=[vm] * len(outs),
        compiler_params=pltpu.CompilerParams(vmem_limit_bytes=VMEM_LIMIT),
    )(*args)


def even(axis):
    at = jnp.int32(0)
    for name in axis if isinstance(axis, tuple) else (axis,):
        at = at * lax.axis_size(name) + lax.axis_index(name)
    return (at & 1) == 0, at


def offsets(spot, own, flag):
    jump = own + HW
    first = jnp.where(flag, spot, spot - jump)
    second = jnp.where(flag, spot - HW - jump, spot - HW)
    return jnp.where(spot < own, spot, jnp.where(spot < own + HW, first, second))


def table_rows(lists_t, counts, first, rows, own, flag):
    width, total = lists_t.shape
    hit = onehot(iota((rows, total), 1) == offsets(iota((rows, total), 0), own, flag) + first)
    entries = lists_t[...]
    coarse = dot_nt(hit, (entries >> 5).astype(F32).astype(BF))
    fine = dot_nt(hit, (entries & 31).astype(F32).astype(BF))
    every = jnp.broadcast_to(counts[...].astype(F32), (128, total)).astype(BF)
    return (coarse * 32.0 + fine).astype(jnp.int32), dot_nt(hit, every)


def list_counts(lists, counts, first, places):
    span = places.shape[1]
    shifted = lists - first
    acc = jnp.zeros(places.shape, F32)
    for k in range(lists.shape[1]):
        hit = (shifted[:, k : k + 1] == places) & (counts[:, :span] > k)
        acc = acc + jnp.where(hit, 1.0, 0.0)
    return acc.astype(BF)


def gather_counts(lists_t, counts_ref, first, own, flag):
    lists, counts = table_rows(lists_t, counts_ref, first, own, own, flag)
    return list_counts(lists, counts, first, offsets(iota((own, own + 2 * HW), 1), own, flag)), counts


def scatter_counts(lists_t, counts_ref, first, own, flag):
    ext = own + 2 * HW
    lists, counts = table_rows(lists_t, counts_ref, first, ext, own, flag)
    return list_counts(lists, counts, first, iota((ext, own), 1))


def wide_sta(mix, target, form, own):
    ext = own + 2 * HW
    step = 128
    per = step // HW
    spread_cols = onehot(iota((ext, ext * HW), 1) >> 4 == iota((ext, ext * HW), 0))
    lane_mask = (iota((step, ext * HW), 0) & 15) == (iota((step, ext * HW), 1) & 15)
    for part in range(own * HW // step):
        pick_rows = onehot((iota((step, own), 0) >> 4) + part * per == iota((step, own), 1))
        full = dot(form(pick_rows, mix).astype(BF), spread_cols)
        target[part * step : (part + 1) * step, :] = jnp.where(lane_mask, full, 0.0).astype(BF)


def src_picks(own):
    return onehot((iota((4 * own, own), 0) & (own - 1)) == iota((4 * own, own), 1))


def wide_src(mix, target, form, own):
    ext = own + 2 * HW
    spread_cols = onehot((iota((ext, 4 * ext), 1) & (ext - 1)) == iota((ext, 4 * ext), 0))
    block_mask = (iota((4 * own, 4 * ext), 0) >> 5) == (iota((4 * own, 4 * ext), 1) >> 6)
    full = dot(form(src_picks(own), mix).astype(BF), spread_cols)
    target[...] = jnp.where(block_mask, full, 0.0).astype(BF)


def doubling(feature):
    channels = 2 * feature
    return onehot((iota((feature, channels), 1) & (feature - 1)) == iota((feature, channels), 0))


def prep0_body(sta_rows, src_rows, slists, scounts, rlists, rcounts, weights, sk, rk, sinv, rinv, wf):
    flag, at = even("sta")
    gather, counts = gather_counts(slists, scounts, at * sta_rows, sta_rows, flag)
    wide_sta(gather, sk, dot, sta_rows)
    pick_rows = onehot((iota((sta_rows * HW, sta_rows), 0) >> 4) == iota((sta_rows * HW, sta_rows), 1))
    sinv[...] = 1.0 / dot(pick_rows, counts.astype(BF))
    flag, at = even(SRC)
    gather, counts = gather_counts(rlists, rcounts, at * src_rows, src_rows, flag)
    wide_src(gather, rk, dot, src_rows)
    rinv[...] = 1.0 / dot(src_picks(src_rows), counts.astype(BF))
    feature = weights.shape[-1]
    channels = 2 * feature
    twice = doubling(feature)
    left = iota((feature, channels), 1) < feature
    for layer in range(LAYERS):
        for which in range(3):
            plain = dot(weights[layer, which], twice)
            at = which * channels
            wf[layer, at : at + feature, :] = jnp.where(left, plain, 0.0).astype(BF)
            wf[layer, at + feature : at + channels, :] = jnp.where(left, 0.0, plain).astype(BF)


def prep1_body(sta_rows, src_rows, _, picks, targets, weights, readout, wb, px, cnt, tgt, rl):
    feature = weights.shape[-1]
    channels = 2 * feature
    unit = onehot(iota((feature, feature), 0) == iota((feature, feature), 1))
    left = iota((feature, channels), 1) < feature
    for layer in range(LAYERS):
        for which in range(3):
            matrix = weights[layer, which]
            turned = dot_nt(unit, jnp.concatenate([matrix, matrix], 0))
            at = which * channels
            wb[layer, :feature, at : at + channels] = jnp.where(left, turned, 0.0).astype(BF)
            wb[layer, feature:, at : at + channels] = jnp.where(left, 0.0, turned).astype(BF)
    twice = doubling(feature)
    rl[...] = dot(jnp.broadcast_to(readout[...].astype(F32), (16, feature)).astype(BF), twice)[:8]

    window = iota((16, sta_rows), 0)
    picked = picks[...].astype(F32)
    rows = jnp.where(window == 0, picked[0:1, :], jnp.where(window == 1, picked[1:2, :], 0.0)).astype(BF)
    choose = onehot((iota((16, channels), 1) >> 6) == iota((16, channels), 0))
    chunk = 256
    for part in range(sta_rows * src_rows // chunk):
        at = part * chunk
        own = onehot((iota((chunk, sta_rows), 0) + at) >> 5 == iota((chunk, sta_rows), 1))
        wide = dot(dot_nt(own, rows).astype(BF), choose).astype(BF)
        span = chunk // src_rows
        px[part * span : (part + 1) * span] = wide.reshape(span, src_rows, channels)
    cnt[...] = dot(rows, jnp.ones((sta_rows, channels), BF))[:8]
    line = iota((8, src_rows), 0)
    aims = targets[...]
    tgt[...] = jnp.where(line == 0, aims[0:1, :], jnp.where(line == 1, aims[1:2, :], 0.0))


def starts(axis, own):
    flag, _ = even(axis)
    last = jnp.int32(own - HW)
    none = jnp.int32(0)
    return [pl.multiple_of(jnp.where(f, last, none), HW) for f in (flag, jnp.logical_not(flag))]


def edge_body(count, *refs):
    x, rest = refs[0], refs[1:count]
    c1, c0, r1, r0 = refs[count : count + 4]
    sems = refs[-1]
    rows, cols, _ = x.shape
    s0, s1 = starts(SRC, cols)
    t0, t1 = starts("sta", rows)
    moves = [(x.at[:, pl.ds(s1, HW)], c1), (x.at[pl.ds(t1, HW)], r1)]
    moves += [(x.at[:, pl.ds(s0, HW)], c0), (x.at[pl.ds(t0, HW)], r0)]
    moves += list(zip(rest, refs[count + 4 : -1]))
    copies = [pltpu.make_async_copy(a, b, sems.at[n]) for n, (a, b) in enumerate(moves)]
    for copy in copies:
        copy.start()
    for copy in copies:
        copy.wait()


def store_edges(by_row, by_col, c1, c0, r1, r0):
    s0, s1 = starts(SRC, by_col.shape[1])
    t0, t1 = starts("sta", by_row.shape[0])
    c1[...] = by_col[:, pl.ds(s1, HW)]
    c0[...] = by_col[:, pl.ds(s0, HW)]
    r1[...] = by_row[pl.ds(t1, HW)]
    r0[...] = by_row[pl.ds(t0, HW)]


def mix_sta(mix, own, r0, r1):
    span = own.shape[0] + 2 * HW
    parts = []
    for g in range(own.shape[1] // HW):
        cut = slice(g * HW, (g + 1) * HW)
        parts.append(jnp.concatenate([own[:, cut], r0[:, cut], r1[:, cut]], 0).reshape(span * HW, 128))
    out = dot(mix[...], jnp.concatenate(parts, 1))
    return [out[:, g * 128 : (g + 1) * 128] for g in range(len(parts))]


def mix_src(mix, own, c0, c1, first):
    parts = []
    for at in (first, first + 4):
        cut = slice(at, at + 4)
        joined = jnp.concatenate([own[cut], c0[cut], c1[cut]], 1)
        parts.append(joined.reshape(4 * joined.shape[1], 128))
    out = dot(mix[...], jnp.concatenate(parts, 1))
    return jnp.concatenate([out[:, :128], out[:, 128:]], 0)


def forward_parts(h, c1, r1, c0, r0, sk, rk, sinv, rinv, wf, states, keep, layer):
    rows, cols, _ = h.shape
    for g, part in enumerate(mix_sta(sk, h, r0, r1)):
        mean = (part * sinv[...]).astype(BF).reshape(rows, HW, 128)
        states[:, g * HW : (g + 1) * HW, 128:256] = mean
    states[:, :, :128] = h[...]
    both = jnp.concatenate([rinv[...], rinv[...]], 0)
    for p in range(rows // 8):
        cut = slice(8 * p, 8 * p + 8)
        mean = (mix_src(rk, h, c0, c1, 8 * p) * both).astype(BF)
        states[cut, :, 256:384] = mean.reshape(8, cols, 128)
        z = dot(states[cut].reshape(8 * cols, 384), wf[layer])
        t = jnp.tanh(z)
        keep[cut] = (1.0 - t * t).reshape(8, cols, 128)
        before = h[cut].reshape(8 * cols, 128).astype(F32)
        yield cut, (before + t).astype(BF)


def forward0_body(h, c1, r1, c0, r0, sk, rk, sinv, rinv, wf, nxt, e1, e0, f1, f0, states, keep):
    cols = h.shape[1]
    for cut, after in forward_parts(h, c1, r1, c0, r0, sk, rk, sinv, rinv, wf, states, keep, 0):
        nxt[cut] = after.reshape(8, cols, 128)
    store_edges(nxt, nxt, e1, e0, f1, f0)


def forward1_body(h, c1, r1, c0, r0, sk, rk, sinv, rinv, wf, px, cnt, rl, states, keep, xsum, block):
    cols = h.shape[1]
    acc = jnp.zeros((cols, 128), F32)
    for cut, after in forward_parts(h, c1, r1, c0, r0, sk, rk, sinv, rinv, wf, states, keep, 1):
        part = after.astype(F32).reshape(8, cols, 128) * px[cut].astype(F32)
        acc = acc + jnp.sum(part, axis=0)
    xsum[...] = acc
    read = jnp.where((iota((8, 128), 1) >> 6) == iota((8, 128), 0), rl[...], 0.0)
    padded = jnp.concatenate([acc, jnp.zeros((128 - cols, 128), F32)], 0)
    sums = dot_nt(read, padded, precision=lax.Precision.HIGHEST)
    mixed = jnp.where(iota((8, 128), 1) < 64, sums, cnt[...])
    block[...] = jnp.broadcast_to(mixed[None], block.shape)


def send_back(p, grad, d, layer, wb, sinv, rinv, direct, usta, usrc):
    cols = usta.shape[1]
    cut = slice(8 * p, 8 * p + 8)
    both = jnp.concatenate([rinv[...], rinv[...]], 0)
    u = dot(d, wb[layer])
    direct[cut] = (grad + u[:, :128]).reshape(8, cols, 128)
    scale = sinv[8 * HW * p : 8 * HW * (p + 1), :].reshape(8, HW, 128)
    scale = jnp.concatenate([scale] * (cols // HW), 1)
    usta[cut] = (u[:, 128:256].reshape(8, cols, 128) * scale).astype(BF)
    usrc[cut] = (u[:, 256:384] * both).astype(BF).reshape(8, cols, 128)


def outer_pairs(states, delta):
    rows, cols, _ = states.shape
    flat = states[...].reshape(rows * cols, 384)
    outer = lax.dot_general(flat, delta[...], TN, preferred_element_type=F32)
    pairs = []
    for which in range(3):
        top = outer[which * 128 : which * 128 + 64]
        low = outer[which * 128 + 64 : which * 128 + 128]
        pairs.append((top + pltpu.roll(low, 64, 1), pltpu.roll(top, 64, 1) + low))
    return pairs


def backward1_body(total, tgt, px, q, rl, wb, sinv, rinv, lik, direct, usta, usrc, e1, e0, f1, f0, errs, delta):
    rows, cols, _ = q.shape
    sums = jnp.sum(total[...], axis=0)
    counts = pltpu.roll(sums, 64, 1)[:, :cols]
    logits = sums[:, :cols] / jnp.sqrt(jnp.maximum(counts, 1.0))
    lik[...] = logits[:2, :]
    error = jax.nn.sigmoid(logits) - tgt[...]
    error = jnp.concatenate([error, jnp.zeros((8, cols), F32)], 0).astype(BF)
    unit = onehot(iota((cols, cols), 0) == iota((cols, cols), 1))
    choose = onehot((iota((16, 128), 1) >> 6) == iota((16, 128), 0))
    wide = dot(dot_nt(unit, error).astype(BF), choose)
    errs[...] = wide
    read = rl[0:1, :]
    for p in range(rows // 8):
        cut = slice(8 * p, 8 * p + 8)
        score = px[cut].astype(F32) * wide[None]
        grad = score.reshape(8 * cols, 128) * read
        d = (grad * q[cut].reshape(8 * cols, 128)).astype(BF)
        delta[8 * cols * p : 8 * cols * (p + 1), :] = d
        send_back(p, grad, d, 1, wb, sinv, rinv, direct, usta, usrc)
    store_edges(usta, usrc, e1, e0, f1, f0)


def weight1_body(states, delta, xsum, errs, slists, scounts, rlists, rcounts, wpart, tk, qk):
    sta_rows, src_rows, _ = states.shape
    flag, at = even("sta")
    wide_sta(scatter_counts(slists, scounts, at * sta_rows, sta_rows, flag), tk, dot_nt, sta_rows)
    flag, at = even(SRC)
    wide_src(scatter_counts(rlists, rcounts, at * src_rows, src_rows, flag), qk, dot_nt, src_rows)
    pairs = outer_pairs(states, delta)
    lane = iota((64, 128), 1) < 64
    wpart[0:64, :] = jnp.where(lane, pairs[0][0], pairs[1][1])
    wpart[64:128, :] = pairs[2][0]
    v = jnp.sum(errs[...] * xsum[...], axis=0, keepdims=True)
    v = jnp.broadcast_to(v, (8, 128))
    wpart[128:136, :] = v + pltpu.roll(v, 64, 1)


def gathered(direct, usta, usrc, c1, r1, c0, r0, tk, qk, hold):
    rows, cols, _ = direct.shape
    for g, part in enumerate(mix_sta(tk, usta, r0, r1)):
        hold[:, g * HW : (g + 1) * HW, :] = part.reshape(rows, HW, 128)

    def make(p):
        cut = slice(8 * p, 8 * p + 8)
        base = (direct[cut] + hold[cut]).reshape(8 * cols, 128)
        return base + mix_src(qk, usrc, c0, c1, 8 * p)

    return make


def backward0_body(direct1, usta1, usrc1, c1, r1, c0, r0, tk, qk, q, states, wb, sinv, rinv, wpart, direct, usta, usrc, e1, e0, f1, f0, pay, delta, hold):
    rows, cols, _ = q.shape
    make = gathered(direct1, usta1, usrc1, c1, r1, c0, r0, tk, qk, hold)
    for p in range(rows // 8):
        grad = make(p)
        d = (grad * q[8 * p : 8 * p + 8].reshape(8 * cols, 128)).astype(BF)
        delta[8 * cols * p : 8 * cols * (p + 1), :] = d
        send_back(p, grad, d, 0, wb, sinv, rinv, direct, usta, usrc)
    store_edges(usta, usrc, e1, e0, f1, f0)
    pairs = outer_pairs(states, delta)
    lane = iota((64, 128), 1) < 64
    pay[0:64, :] = wpart[0:64, :]
    pay[64:128, :] = jnp.where(lane, wpart[64:128, :], pairs[2][1])
    pay[128:192, :] = jnp.where(lane, pairs[0][0], pairs[1][1])
    pay[192:200, :] = wpart[128:136, :]
    pay[200:, :] = jnp.zeros((pay.shape[0] - 200, 128), F32)


def last_body(direct, usta, usrc, c1, r1, c0, r0, tk, qk, out, hold):
    make = gathered(direct, usta, usrc, c1, r1, c0, r0, tk, qk, hold)
    cols = direct.shape[1]
    for p in range(direct.shape[0] // 8):
        out[8 * p : 8 * p + 8] = make(p).astype(BF).reshape(8, cols, 128)


def sum_body(x, out):
    total = jnp.sum(x[...].astype(F32), axis=0).astype(out.dtype)
    out[...] = jnp.broadcast_to(total[None], out.shape)


def unpack_body(factor, x, w, v):
    flat = x[...].astype(F32).reshape(-1, 128) * factor
    first = flat[0:64]
    second = flat[64:128]
    third = flat[128:192]
    w[1, 0] = first[:, :64]
    w[1, 1] = pltpu.roll(first, 64, 1)[:, :64]
    w[1, 2] = second[:, :64]
    w[0, 2] = pltpu.roll(second, 64, 1)[:, :64]
    w[0, 0] = third[:, :64]
    w[0, 1] = pltpu.roll(third, 64, 1)[:, :64]
    v[...] = flat[192:193, :64]


def scratch_call(body, outs, scratch, *args, away=0):
    vm = pl.BlockSpec(memory_space=pltpu.VMEM)
    args = [pltpu.with_memory_space_constraint(x, pltpu.HBM) if n < away else x for n, x in enumerate(args)]
    return pl.pallas_call(
        body,
        out_shape=[jax.ShapeDtypeStruct(s, d) for s, d in outs],
        in_specs=[pl.BlockSpec(memory_space=pltpu.HBM)] * away + [vm] * (len(args) - away),
        out_specs=[vm] * len(outs),
        scratch_shapes=scratch,
        compiler_params=pltpu.CompilerParams(vmem_limit_bytes=VMEM_LIMIT),
    )(*args)


def pairs_of(axis):
    count = 1
    for name in axis if isinstance(axis, tuple) else (axis,):
        count *= lax.axis_size(name)
    inner = [(i, i ^ 1) for i in range(count)]
    outer = [(i, ((i + 1) ^ 1) - 1) for i in range(1, count - 1)]
    return inner, outer


def halo(e1, e0, f1, f0):
    src0, src1 = pairs_of(SRC)
    sta0, sta1 = pairs_of("sta")
    return (
        lax.ppermute(e1, SRC, src1),
        lax.ppermute(f1, "sta", sta1),
        lax.ppermute(e0, SRC, src0),
        lax.ppermute(f0, "sta", sta0),
    )


def shards(features, station_lists, station_counts, source_lists, source_counts, picks, targets, layer_weights, readout_vector):
    rows, cols, channels = features.shape
    n_sta = lax.axis_size("sta")
    n_z = lax.axis_size("z")
    n_plane = n_sta * lax.axis_size("xh")
    whole = (rows, cols, channels)
    edge_outs = [((rows, HW, channels), BF)] * 2 + [((HW, cols, channels), BF)] * 2
    ext_sta, ext_src = rows + 2 * HW, cols + 2 * HW
    tables = (station_lists.T, station_counts.reshape(1, -1), source_lists.T, source_counts.reshape(1, -1))

    small = tables + (layer_weights, picks, targets, readout_vector.reshape(1, -1))
    c1, c0, r1, r0, *small = scratch_call(
        lambda *refs: edge_body(1 + len(small), *refs),
        edge_outs + [(x.shape, x.dtype) for x in small],
        [pltpu.SemaphoreType.DMA((4 + len(small),))],
        features,
        *small,
        away=1 + len(small),
    )
    edges = (c1, c0, r1, r0)
    tables, (weights, picks, targets, readout) = small[:4], small[4:]
    sk, rk, sinv, rinv, wf = scratch_call(
        lambda *refs: prep0_body(rows, cols, *refs),
        [
            ((rows * HW, ext_sta * HW), BF),
            ((4 * cols, 4 * ext_src), BF),
            ((rows * HW, channels), F32),
            ((4 * cols, channels), F32),
            ((LAYERS, 3 * channels, channels), BF),
        ],
        [],
        *tables,
        weights,
    )
    state_outs = [((rows, cols, 3 * channels), BF), (whole, F32)]
    h1, *edges, states0, q0 = call(
        forward0_body, [(whole, BF)] + edge_outs + state_outs, features, *halo(*edges), sk, rk, sinv, rinv, wf
    )
    wb, px, cnt, tgt, rl = scratch_call(
        lambda *refs: prep1_body(rows, cols, *refs),
        [
            ((LAYERS, channels, 3 * channels), BF),
            (whole, BF),
            ((8, channels), F32),
            ((8, cols), F32),
            ((8, channels), F32),
        ],
        [],
        states0,
        picks,
        targets,
        weights,
        readout,
    )
    states1, q1, xsum, block = call(
        forward1_body,
        state_outs + [((cols, channels), F32), ((n_sta, 8, channels), F32)],
        h1,
        *halo(*edges),
        sk,
        rk,
        sinv,
        rinv,
        wf,
        px,
        cnt,
        rl,
    )
    total = lax.all_to_all(block, "sta", 0, 0)
    grad_outs = [(whole, F32), (whole, BF), (whole, BF)] + edge_outs
    flat = ((rows * cols, channels), BF)
    likelihood, direct, usta, usrc, *edges, errs, delta = call(
        backward1_body,
        [((2, cols), F32)] + grad_outs + [((cols, channels), F32), flat],
        total,
        tgt,
        px,
        q1,
        rl,
        wb,
        sinv,
        rinv,
    )
    wpart, tk, qk = call(
        weight1_body,
        [((136, channels), F32), ((rows * HW, ext_sta * HW), BF), ((4 * cols, 4 * ext_src), BF)],
        states1,
        delta,
        xsum,
        errs,
        *tables,
    )
    per = -(-200 // (8 * n_plane)) * 8
    direct, usta, usrc, *edges, pay = scratch_call(
        backward0_body,
        grad_outs + [((per * n_plane, channels), F32)],
        [pltpu.VMEM(*flat), pltpu.VMEM(whole, F32)],
        direct,
        usta,
        usrc,
        *halo(*edges),
        tk,
        qk,
        q0,
        states0,
        wb,
        sinv,
        rinv,
        wpart,
    )
    (feature_grad,) = scratch_call(
        last_body, [(whole, BF)], [pltpu.VMEM(whole, F32)], direct, usta, usrc, *halo(*edges), tk, qk
    )
    part = lax.all_to_all(pay.reshape(n_plane, per, channels), PLANE, 0, 0)
    (part,) = call(sum_body, [((n_z, per, channels), BF)], part)
    part = lax.all_to_all(part, "z", 0, 0)
    (part,) = call(sum_body, [((n_plane, per, channels), BF)], part)
    part = lax.all_to_all(part, PLANE, 0, 0)
    nodes = float(rows * n_sta * cols * lax.axis_size("z") * lax.axis_size("xh"))
    feature = layer_weights.shape[-1]
    weight_grad, vector_grad = call(
        lambda *refs: unpack_body(nodes**-0.5, *refs),
        [(layer_weights.shape, F32), ((1, feature), F32)],
        part,
    )
    return likelihood, feature_grad, weight_grad, vector_grad.reshape(feature)


def solution(mesh):
    n_sta, n_src = mesh.devices.shape
    near = 2
    fine = Mesh(mesh.devices.reshape(n_sta, n_src // near, near), ("sta",) + SRC)
    in_specs = (P("sta", SRC, None), P(), P(), P(), P(), P(None, "sta"), P(None, SRC), P(), P())
    out_specs = (P(None, SRC), P("sta", SRC, None), P(), P())
    return jax.shard_map(shards, mesh=fine, in_specs=in_specs, out_specs=out_specs, check_vma=False)
```

```python
import jax
import jax.numpy as jnp
from jax import lax
from jax.experimental import pallas as pl
from jax.experimental.pallas import tpu as pltpu
from jax.sharding import Mesh
from jax.sharding import PartitionSpec as P

LAYERS = 2
HW = 16
BF = jnp.bfloat16
F32 = jnp.float32
PLANE = ("sta", "xh")
SRC = ("z", "xh")
NT = (((1,), (1,)), ((), ()))
TN = (((0,), (0,)), ((), ()))
VMEM_LIMIT = 16 * 1024 * 1024


def iota(shape, dim):
    return lax.broadcasted_iota(jnp.int32, shape, dim)


def dot(a, b):
    return jnp.dot(a, b, preferred_element_type=F32)


def dot_nt(a, b, precision=None):
    return lax.dot_general(a, b, NT, precision=precision, preferred_element_type=F32)


def onehot(mask):
    return jnp.where(mask, 1.0, 0.0).astype(BF)


def call(body, outs, *args):
    vm = pl.BlockSpec(memory_space=pltpu.VMEM)
    return pl.pallas_call(
        body,
        out_shape=[jax.ShapeDtypeStruct(s, d) for s, d in outs],
        in_specs=[vm] * len(args),
        out_specs=[vm] * len(outs),
        compiler_params=pltpu.CompilerParams(vmem_limit_bytes=VMEM_LIMIT),
    )(*args)


def even(axis):
    at = jnp.int32(0)
    for name in axis if isinstance(axis, tuple) else (axis,):
        at = at * lax.axis_size(name) + lax.axis_index(name)
    return (at & 1) == 0, at


def offsets(spot, own, flag):
    jump = own + HW
    first = jnp.where(flag, spot, spot - jump)
    second = jnp.where(flag, spot - HW - jump, spot - HW)
    return jnp.where(spot < own, spot, jnp.where(spot < own + HW, first, second))


def table_rows(lists_t, counts, first, rows, own, flag):
    width, total = lists_t.shape
    hit = onehot(iota((rows, total), 1) == offsets(iota((rows, total), 0), own, flag) + first)
    entries = lists_t[...]
    coarse = dot_nt(hit, (entries >> 5).astype(F32).astype(BF))
    fine = dot_nt(hit, (entries & 31).astype(F32).astype(BF))
    every = jnp.broadcast_to(counts[...].astype(F32), (128, total)).astype(BF)
    return (coarse * 32.0 + fine).astype(jnp.int32), dot_nt(hit, every)


def list_counts(lists, counts, first, places):
    span = places.shape[1]
    shifted = lists - first
    acc = jnp.zeros(places.shape, F32)
    for k in range(lists.shape[1]):
        hit = (shifted[:, k : k + 1] == places) & (counts[:, :span] > k)
        acc = acc + jnp.where(hit, 1.0, 0.0)
    return acc.astype(BF)


def gather_counts(lists_t, counts_ref, first, own, flag):
    lists, counts = table_rows(lists_t, counts_ref, first, own, own, flag)
    return list_counts(lists, counts, first, offsets(iota((own, own + 2 * HW), 1), own, flag)), counts


def scatter_counts(lists_t, counts_ref, first, own, flag):
    ext = own + 2 * HW
    lists, counts = table_rows(lists_t, counts_ref, first, ext, own, flag)
    return list_counts(lists, counts, first, iota((ext, own), 1))


def wide_sta(mix, target, form, own):
    ext = own + 2 * HW
    step = 128
    per = step // HW
    spread_cols = onehot(iota((ext, ext * HW), 1) >> 4 == iota((ext, ext * HW), 0))
    lane_mask = (iota((step, ext * HW), 0) & 15) == (iota((step, ext * HW), 1) & 15)
    for part in range(own * HW // step):
        pick_rows = onehot((iota((step, own), 0) >> 4) + part * per == iota((step, own), 1))
        full = dot(form(pick_rows, mix).astype(BF), spread_cols)
        target[part * step : (part + 1) * step, :] = jnp.where(lane_mask, full, 0.0).astype(BF)


def src_picks(own):
    return onehot((iota((4 * own, own), 0) & (own - 1)) == iota((4 * own, own), 1))


def wide_src(mix, target, form, own):
    ext = own + 2 * HW
    spread_cols = onehot((iota((ext, 4 * ext), 1) & (ext - 1)) == iota((ext, 4 * ext), 0))
    block_mask = (iota((4 * own, 4 * ext), 0) >> 5) == (iota((4 * own, 4 * ext), 1) >> 6)
    full = dot(form(src_picks(own), mix).astype(BF), spread_cols)
    target[...] = jnp.where(block_mask, full, 0.0).astype(BF)


def doubling(feature):
    channels = 2 * feature
    return onehot((iota((feature, channels), 1) & (feature - 1)) == iota((feature, channels), 0))


def prep0_body(sta_rows, src_rows, slists, scounts, rlists, rcounts, weights, sk, rk, sinv, rinv, wf, tk, qk):
    flag, at = even("sta")
    wide_sta(scatter_counts(slists, scounts, at * sta_rows, sta_rows, flag), tk, dot_nt, sta_rows)
    flag, at = even(SRC)
    wide_src(scatter_counts(rlists, rcounts, at * src_rows, src_rows, flag), qk, dot_nt, src_rows)
    flag, at = even("sta")
    gather, counts = gather_counts(slists, scounts, at * sta_rows, sta_rows, flag)
    wide_sta(gather, sk, dot, sta_rows)
    pick_rows = onehot((iota((sta_rows * HW, sta_rows), 0) >> 4) == iota((sta_rows * HW, sta_rows), 1))
    sinv[...] = 1.0 / dot(pick_rows, counts.astype(BF))
    flag, at = even(SRC)
    gather, counts = gather_counts(rlists, rcounts, at * src_rows, src_rows, flag)
    wide_src(gather, rk, dot, src_rows)
    rinv[...] = 1.0 / dot(src_picks(src_rows), counts.astype(BF))
    feature = weights.shape[-1]
    channels = 2 * feature
    twice = doubling(feature)
    left = iota((feature, channels), 1) < feature
    for layer in range(LAYERS):
        for which in range(3):
            plain = dot(weights[layer, which], twice)
            at = which * channels
            wf[layer, at : at + feature, :] = jnp.where(left, plain, 0.0).astype(BF)
            wf[layer, at + feature : at + channels, :] = jnp.where(left, 0.0, plain).astype(BF)


def prep1_body(sta_rows, src_rows, _, picks, targets, weights, readout, wb, px, cnt, tgt, rl):
    feature = weights.shape[-1]
    channels = 2 * feature
    unit = onehot(iota((feature, feature), 0) == iota((feature, feature), 1))
    left = iota((feature, channels), 1) < feature
    for layer in range(LAYERS):
        for which in range(3):
            matrix = weights[layer, which]
            turned = dot_nt(unit, jnp.concatenate([matrix, matrix], 0))
            at = which * channels
            wb[layer, :feature, at : at + channels] = jnp.where(left, turned, 0.0).astype(BF)
            wb[layer, feature:, at : at + channels] = jnp.where(left, 0.0, turned).astype(BF)
    twice = doubling(feature)
    rl[...] = dot(jnp.broadcast_to(readout[...].astype(F32), (16, feature)).astype(BF), twice)[:8]

    window = iota((16, sta_rows), 0)
    picked = picks[...].astype(F32)
    rows = jnp.where(window == 0, picked[0:1, :], jnp.where(window == 1, picked[1:2, :], 0.0)).astype(BF)
    choose = onehot((iota((16, channels), 1) >> 6) == iota((16, channels), 0))
    chunk = 256
    for part in range(sta_rows * src_rows // chunk):
        at = part * chunk
        own = onehot((iota((chunk, sta_rows), 0) + at) >> 5 == iota((chunk, sta_rows), 1))
        wide = dot(dot_nt(own, rows).astype(BF), choose).astype(BF)
        span = chunk // src_rows
        px[part * span : (part + 1) * span] = wide.reshape(span, src_rows, channels)
    cnt[...] = dot(rows, jnp.ones((sta_rows, channels), BF))[:8]
    line = iota((8, src_rows), 0)
    aims = targets[...]
    tgt[...] = jnp.where(line == 0, aims[0:1, :], jnp.where(line == 1, aims[1:2, :], 0.0))


def starts(axis, own):
    flag, _ = even(axis)
    last = jnp.int32(own - HW)
    none = jnp.int32(0)
    return [pl.multiple_of(jnp.where(f, last, none), HW) for f in (flag, jnp.logical_not(flag))]


def edge_body(count, *refs):
    x, rest = refs[0], refs[1:count]
    c1, c0, r1, r0 = refs[count : count + 4]
    sems = refs[-1]
    rows, cols, _ = x.shape
    s0, s1 = starts(SRC, cols)
    t0, t1 = starts("sta", rows)
    moves = [(x.at[:, pl.ds(s1, HW)], c1), (x.at[pl.ds(t1, HW)], r1)]
    moves += [(x.at[:, pl.ds(s0, HW)], c0), (x.at[pl.ds(t0, HW)], r0)]
    moves += list(zip(rest, refs[count + 4 : -1]))
    copies = [pltpu.make_async_copy(a, b, sems.at[n]) for n, (a, b) in enumerate(moves)]
    for copy in copies:
        copy.start()
    for copy in copies:
        copy.wait()


def store_edges(by_row, by_col, c1, c0, r1, r0):
    s0, s1 = starts(SRC, by_col.shape[1])
    t0, t1 = starts("sta", by_row.shape[0])
    c1[...] = by_col[:, pl.ds(s1, HW)]
    c0[...] = by_col[:, pl.ds(s0, HW)]
    r1[...] = by_row[pl.ds(t1, HW)]
    r0[...] = by_row[pl.ds(t0, HW)]


def mix_sta(mix, own, r0, r1):
    span = own.shape[0] + 2 * HW
    parts = []
    for g in range(own.shape[1] // HW):
        cut = slice(g * HW, (g + 1) * HW)
        parts.append(jnp.concatenate([own[:, cut], r0[:, cut], r1[:, cut]], 0).reshape(span * HW, 128))
    out = dot(mix[...], jnp.concatenate(parts, 1))
    return [out[:, g * 128 : (g + 1) * 128] for g in range(len(parts))]


def mix_src(mix, own, c0, c1, first):
    parts = []
    for at in (first, first + 4):
        cut = slice(at, at + 4)
        joined = jnp.concatenate([own[cut], c0[cut], c1[cut]], 1)
        parts.append(joined.reshape(4 * joined.shape[1], 128))
    out = dot(mix[...], jnp.concatenate(parts, 1))
    return jnp.concatenate([out[:, :128], out[:, 128:]], 0)


def forward_parts(h, c1, r1, c0, r0, sk, rk, sinv, rinv, wf, states, keep, layer):
    rows, cols, _ = h.shape
    for g, part in enumerate(mix_sta(sk, h, r0, r1)):
        mean = (part * sinv[...]).astype(BF).reshape(rows, HW, 128)
        states[:, g * HW : (g + 1) * HW, 128:256] = mean
    states[:, :, :128] = h[...]
    both = jnp.concatenate([rinv[...], rinv[...]], 0)
    for p in range(rows // 8):
        cut = slice(8 * p, 8 * p + 8)
        mean = (mix_src(rk, h, c0, c1, 8 * p) * both).astype(BF)
        states[cut, :, 256:384] = mean.reshape(8, cols, 128)
        z = dot(states[cut].reshape(8 * cols, 384), wf[layer])
        t = jnp.tanh(z)
        keep[cut] = (1.0 - t * t).reshape(8, cols, 128)
        before = h[cut].reshape(8 * cols, 128).astype(F32)
        yield cut, (before + t).astype(BF)


def forward0_body(h, c1, r1, c0, r0, sk, rk, sinv, rinv, wf, nxt, e1, e0, f1, f0, states, keep):
    cols = h.shape[1]
    for cut, after in forward_parts(h, c1, r1, c0, r0, sk, rk, sinv, rinv, wf, states, keep, 0):
        nxt[cut] = after.reshape(8, cols, 128)
    store_edges(nxt, nxt, e1, e0, f1, f0)


def forward1_body(h, c1, r1, c0, r0, sk, rk, sinv, rinv, wf, px, cnt, rl, states, keep, xsum, block):
    cols = h.shape[1]
    acc = jnp.zeros((cols, 128), F32)
    for cut, after in forward_parts(h, c1, r1, c0, r0, sk, rk, sinv, rinv, wf, states, keep, 1):
        part = after.astype(F32).reshape(8, cols, 128) * px[cut].astype(F32)
        acc = acc + jnp.sum(part, axis=0)
    xsum[...] = acc
    read = jnp.where((iota((8, 128), 1) >> 6) == iota((8, 128), 0), rl[...], 0.0)
    padded = jnp.concatenate([acc, jnp.zeros((128 - cols, 128), F32)], 0)
    sums = dot_nt(read, padded, precision=lax.Precision.HIGHEST)
    mixed = jnp.where(iota((8, 128), 1) < 64, sums, cnt[...])
    block[...] = jnp.broadcast_to(mixed[None], block.shape)


def send_back(p, grad, d, layer, wb, sinv, rinv, direct, usta, usrc):
    cols = usta.shape[1]
    cut = slice(8 * p, 8 * p + 8)
    both = jnp.concatenate([rinv[...], rinv[...]], 0)
    u = dot(d, wb[layer])
    direct[cut] = (grad + u[:, :128]).reshape(8, cols, 128)
    scale = sinv[8 * HW * p : 8 * HW * (p + 1), :].reshape(8, HW, 128)
    scale = jnp.concatenate([scale] * (cols // HW), 1)
    usta[cut] = (u[:, 128:256].reshape(8, cols, 128) * scale).astype(BF)
    usrc[cut] = (u[:, 256:384] * both).astype(BF).reshape(8, cols, 128)


def outer_pairs(states, delta):
    rows, cols, _ = states.shape
    flat = states[...].reshape(rows * cols, 384)
    outer = lax.dot_general(flat, delta[...], TN, preferred_element_type=F32)
    pairs = []
    for which in range(3):
        top = outer[which * 128 : which * 128 + 64]
        low = outer[which * 128 + 64 : which * 128 + 128]
        pairs.append((top + pltpu.roll(low, 64, 1), pltpu.roll(top, 64, 1) + low))
    return pairs


def backward1_body(total, tgt, px, q, rl, wb, sinv, rinv, lik, direct, usta, usrc, e1, e0, f1, f0, errs, delta):
    rows, cols, _ = q.shape
    sums = jnp.sum(total[...], axis=0)
    counts = pltpu.roll(sums, 64, 1)[:, :cols]
    logits = sums[:, :cols] / jnp.sqrt(jnp.maximum(counts, 1.0))
    lik[...] = logits[:2, :]
    error = jax.nn.sigmoid(logits) - tgt[...]
    error = jnp.concatenate([error, jnp.zeros((8, cols), F32)], 0).astype(BF)
    unit = onehot(iota((cols, cols), 0) == iota((cols, cols), 1))
    choose = onehot((iota((16, 128), 1) >> 6) == iota((16, 128), 0))
    wide = dot(dot_nt(unit, error).astype(BF), choose)
    errs[...] = wide
    read = rl[0:1, :]
    for p in range(rows // 8):
        cut = slice(8 * p, 8 * p + 8)
        score = px[cut].astype(F32) * wide[None]
        grad = score.reshape(8 * cols, 128) * read
        d = (grad * q[cut].reshape(8 * cols, 128)).astype(BF)
        delta[8 * cols * p : 8 * cols * (p + 1), :] = d
        send_back(p, grad, d, 1, wb, sinv, rinv, direct, usta, usrc)
    store_edges(usta, usrc, e1, e0, f1, f0)


def weight1_body(states, delta, xsum, errs, wpart):
    pairs = outer_pairs(states, delta)
    lane = iota((64, 128), 1) < 64
    wpart[0:64, :] = jnp.where(lane, pairs[0][0], pairs[1][1])
    wpart[64:128, :] = pairs[2][0]
    v = jnp.sum(errs[...] * xsum[...], axis=0, keepdims=True)
    v = jnp.broadcast_to(v, (8, 128))
    wpart[128:136, :] = v + pltpu.roll(v, 64, 1)


def gathered(direct, usta, usrc, c1, r1, c0, r0, tk, qk, hold):
    rows, cols, _ = direct.shape
    for g, part in enumerate(mix_sta(tk, usta, r0, r1)):
        hold[:, g * HW : (g + 1) * HW, :] = part.reshape(rows, HW, 128)

    def make(p):
        cut = slice(8 * p, 8 * p + 8)
        base = (direct[cut] + hold[cut]).reshape(8 * cols, 128)
        return base + mix_src(qk, usrc, c0, c1, 8 * p)

    return make


def backward0_body(direct1, usta1, usrc1, c1, r1, c0, r0, tk, qk, q, states, wb, sinv, rinv, wpart, direct, usta, usrc, e1, e0, f1, f0, pay, delta, hold):
    rows, cols, _ = q.shape
    make = gathered(direct1, usta1, usrc1, c1, r1, c0, r0, tk, qk, hold)
    for p in range(rows // 8):
        grad = make(p)
        d = (grad * q[8 * p : 8 * p + 8].reshape(8 * cols, 128)).astype(BF)
        delta[8 * cols * p : 8 * cols * (p + 1), :] = d
        send_back(p, grad, d, 0, wb, sinv, rinv, direct, usta, usrc)
    store_edges(usta, usrc, e1, e0, f1, f0)
    pairs = outer_pairs(states, delta)
    lane = iota((64, 128), 1) < 64
    pay[0:64, :] = wpart[0:64, :]
    pay[64:128, :] = jnp.where(lane, wpart[64:128, :], pairs[2][1])
    pay[128:192, :] = jnp.where(lane, pairs[0][0], pairs[1][1])
    pay[192:200, :] = wpart[128:136, :]
    pay[200:, :] = jnp.zeros((pay.shape[0] - 200, 128), F32)


def last_body(direct, usta, usrc, c1, r1, c0, r0, tk, qk, out, hold):
    make = gathered(direct, usta, usrc, c1, r1, c0, r0, tk, qk, hold)
    cols = direct.shape[1]
    for p in range(direct.shape[0] // 8):
        out[8 * p : 8 * p + 8] = make(p).astype(BF).reshape(8, cols, 128)


def sum_body(x, out):
    out[...] = jnp.broadcast_to(jnp.sum(x[...], axis=0)[None], out.shape)


def unpack_body(factor, x, w, v):
    flat = x[...].reshape(-1, 128) * factor
    first = flat[0:64]
    second = flat[64:128]
    third = flat[128:192]
    w[1, 0] = first[:, :64]
    w[1, 1] = pltpu.roll(first, 64, 1)[:, :64]
    w[1, 2] = second[:, :64]
    w[0, 2] = pltpu.roll(second, 64, 1)[:, :64]
    w[0, 0] = third[:, :64]
    w[0, 1] = pltpu.roll(third, 64, 1)[:, :64]
    v[...] = flat[192:193, :64]


def scratch_call(body, outs, scratch, *args, away=0):
    vm = pl.BlockSpec(memory_space=pltpu.VMEM)
    args = [pltpu.with_memory_space_constraint(x, pltpu.HBM) if n < away else x for n, x in enumerate(args)]
    return pl.pallas_call(
        body,
        out_shape=[jax.ShapeDtypeStruct(s, d) for s, d in outs],
        in_specs=[pl.BlockSpec(memory_space=pltpu.HBM)] * away + [vm] * (len(args) - away),
        out_specs=[vm] * len(outs),
        scratch_shapes=scratch,
        compiler_params=pltpu.CompilerParams(vmem_limit_bytes=VMEM_LIMIT),
    )(*args)


def pairs_of(axis):
    count = 1
    for name in axis if isinstance(axis, tuple) else (axis,):
        count *= lax.axis_size(name)
    inner = [(i, i ^ 1) for i in range(count)]
    outer = [(i, ((i + 1) ^ 1) - 1) for i in range(1, count - 1)]
    return inner, outer


def halo(e1, e0, f1, f0):
    src0, src1 = pairs_of(SRC)
    sta0, sta1 = pairs_of("sta")
    return (
        lax.ppermute(e1, SRC, src1),
        lax.ppermute(f1, "sta", sta1),
        lax.ppermute(e0, SRC, src0),
        lax.ppermute(f0, "sta", sta0),
    )


def shards(features, station_lists, station_counts, source_lists, source_counts, picks, targets, layer_weights, readout_vector):
    rows, cols, channels = features.shape
    n_sta = lax.axis_size("sta")
    n_z = lax.axis_size("z")
    n_plane = n_sta * lax.axis_size("xh")
    whole = (rows, cols, channels)
    edge_outs = [((rows, HW, channels), BF)] * 2 + [((HW, cols, channels), BF)] * 2
    ext_sta, ext_src = rows + 2 * HW, cols + 2 * HW
    tables = (station_lists.T, station_counts.reshape(1, -1), source_lists.T, source_counts.reshape(1, -1))

    small = tables + (layer_weights, picks, targets, readout_vector.reshape(1, -1))
    c1, c0, r1, r0, *small = scratch_call(
        lambda *refs: edge_body(1 + len(small), *refs),
        edge_outs + [(x.shape, x.dtype) for x in small],
        [pltpu.SemaphoreType.DMA((4 + len(small),))],
        features,
        *small,
        away=1 + len(small),
    )
    edges = (c1, c0, r1, r0)
    tables, (weights, picks, targets, readout) = small[:4], small[4:]
    sk, rk, sinv, rinv, wf, tk, qk = scratch_call(
        lambda *refs: prep0_body(rows, cols, *refs),
        [
            ((rows * HW, ext_sta * HW), BF),
            ((4 * cols, 4 * ext_src), BF),
            ((rows * HW, channels), F32),
            ((4 * cols, channels), F32),
            ((LAYERS, 3 * channels, channels), BF),
            ((rows * HW, ext_sta * HW), BF),
            ((4 * cols, 4 * ext_src), BF),
        ],
        [],
        *tables,
        weights,
    )
    state_outs = [((rows, cols, 3 * channels), BF), (whole, F32)]
    h1, *edges, states0, q0 = call(
        forward0_body, [(whole, BF)] + edge_outs + state_outs, features, *halo(*edges), sk, rk, sinv, rinv, wf
    )
    wb, px, cnt, tgt, rl = scratch_call(
        lambda *refs: prep1_body(rows, cols, *refs),
        [
            ((LAYERS, channels, 3 * channels), BF),
            (whole, BF),
            ((8, channels), F32),
            ((8, cols), F32),
            ((8, channels), F32),
        ],
        [],
        states0,
        picks,
        targets,
        weights,
        readout,
    )
    states1, q1, xsum, block = call(
        forward1_body,
        state_outs + [((cols, channels), F32), ((n_sta, 8, channels), F32)],
        h1,
        *halo(*edges),
        sk,
        rk,
        sinv,
        rinv,
        wf,
        px,
        cnt,
        rl,
    )
    total = lax.all_to_all(block, "sta", 0, 0)
    grad_outs = [(whole, F32), (whole, BF), (whole, BF)] + edge_outs
    flat = ((rows * cols, channels), BF)
    likelihood, direct, usta, usrc, *edges, errs, delta = call(
        backward1_body,
        [((2, cols), F32)] + grad_outs + [((cols, channels), F32), flat],
        total,
        tgt,
        px,
        q1,
        rl,
        wb,
        sinv,
        rinv,
    )
    (wpart,) = call(weight1_body, [((136, channels), F32)], states1, delta, xsum, errs)
    per = -(-200 // (8 * n_plane)) * 8
    direct, usta, usrc, *edges, pay = scratch_call(
        backward0_body,
        grad_outs + [((per * n_plane, channels), F32)],
        [pltpu.VMEM(*flat), pltpu.VMEM(whole, F32)],
        direct,
        usta,
        usrc,
        *halo(*edges),
        tk,
        qk,
        q0,
        states0,
        wb,
        sinv,
        rinv,
        wpart,
    )
    (feature_grad,) = scratch_call(
        last_body, [(whole, BF)], [pltpu.VMEM(whole, F32)], direct, usta, usrc, *halo(*edges), tk, qk
    )
    part = lax.all_to_all(pay.reshape(n_plane, per, channels), PLANE, 0, 0)
    (part,) = call(sum_body, [((n_z, per, channels), F32)], part)
    part = lax.all_to_all(part, "z", 0, 0)
    (part,) = call(sum_body, [((n_plane, per, channels), F32)], part)
    part = lax.all_to_all(part, PLANE, 0, 0)
    nodes = float(rows * n_sta * cols * lax.axis_size("z") * lax.axis_size("xh"))
    feature = layer_weights.shape[-1]
    weight_grad, vector_grad = call(
        lambda *refs: unpack_body(nodes**-0.5, *refs),
        [(layer_weights.shape, F32), ((1, feature), F32)],
        part,
    )
    return likelihood, feature_grad, weight_grad, vector_grad.reshape(feature)


def solution(mesh):
    n_sta, n_src = mesh.devices.shape
    near = 2
    fine = Mesh(mesh.devices.reshape(n_sta, n_src // near, near), ("sta",) + SRC)
    in_specs = (P("sta", SRC, None), P(), P(), P(), P(), P(None, "sta"), P(None, SRC), P(), P())
    out_specs = (P(None, SRC), P("sta", SRC, None), P(), P())
    return jax.shard_map(shards, mesh=fine, in_specs=in_specs, out_specs=out_specs, check_vma=False)
```
